32 devices in a mesh: rows: 8 (over z, y), cols: 4 (over x, core).
Axes of the slice: x: 2, y: 2, z: 4, core: 2. Of those that a mesh axis runs over, the one named last changes fastest.
Arguments:
- basis_cols: bfloat16 [32768, 1024], P('rows', 'cols'), may hold values from -6 to 6, as said below
- snapshots: bfloat16 [256, 32768], P(None, 'rows'), may hold values from -600 to 600
Outputs:
- coefficients: float32 [1024, 256], P('cols')
- factor: float32 [256, 256], replicated
- directions: bfloat16 [256, 32768], P(None, ('rows', 'cols'))
The draws below stay inside these ranges and needn't reach their ends.
Inputs may be any that keep to these rules, and one draw needn't show every extreme that they name: `basis_cols`: normal entries.
All inputs are finite; a program needn't handle non-finite values.
Results may differ from the reference program's by a relative error of at most 0.0056.
Values may be sent and summed in bfloat16 or wider, within the bound.
No kernel may reach another device: no remote copies, remote signals or barrier semaphores. Data moves between devices by JAX's collectives and lax.ppermute only.
A program may use at most 64 MiB of HBM per device.

```python
import math
import jax
import jax.numpy as jnp
from jax import lax

RANK = 1024
SNAPS = 256
M_DEV = 4096
M = 32768


def basis_block(key, index):
    sub = jax.random.fold_in(jax.random.fold_in(key, 7), index)
    return jnp.clip(jax.random.normal(sub, (M_DEV, RANK), jnp.float32), -6.0, 6.0)


def draw_basis_cols(key, part):
    blocks = lax.map(lambda index: basis_block(key, index).astype(jnp.bfloat16), jnp.arange(M // M_DEV))
    return blocks.reshape(M, RANK)


def draw_snapshots(key, part):
    amp_key = jax.random.fold_in(key, 11)
    amplitude = jax.random.normal(jax.random.fold_in(amp_key, 1), (RANK, SNAPS), jnp.float32)
    snap_scale = jnp.exp(jax.random.uniform(jax.random.fold_in(amp_key, 2), (SNAPS,), jnp.float32) * math.log(10.0))
    amplitude = amplitude * snap_scale[None, :]

    def one_block(index):
        lower = basis_block(key, index)
        signal = jnp.dot(lower, amplitude, precision=lax.Precision.HIGHEST) / math.sqrt(RANK)
        noise_key = jax.random.fold_in(jax.random.fold_in(key, 13), index)
        noise = jax.random.normal(noise_key, (M_DEV, SNAPS), jnp.float32)
        points = (index * M_DEV + jnp.arange(M_DEV)).astype(jnp.float32)
        row_key = jax.random.fold_in(jax.random.fold_in(key, 17), index)
        rise = jnp.exp(math.log(3.0) * points / M) * jnp.exp(jax.random.uniform(row_key, (M_DEV,), jnp.float32) * math.log(4.0))
        return (rise[:, None] * (signal + 0.5 * snap_scale[None, :] * noise)).T
    blocks = lax.map(one_block, jnp.arange(M // M_DEV))
    whole = jnp.transpose(blocks, (1, 0, 2)).reshape(SNAPS, M)
    return jnp.clip(whole, -600.0, 600.0).astype(jnp.bfloat16)


def setup_inputs(seed: int = 0) -> dict:
    streams_of = jax.random.split(jax.random.key(seed), 3)
    return {
        "basis_cols": draw_basis_cols(jax.random.fold_in(streams_of[2], 71), 0),
        "snapshots": draw_snapshots(jax.random.fold_in(streams_of[2], 71), 0),
    }


def reference(basis_cols, snapshots):
    raw = lax.dot_general(basis_cols.astype(jnp.float32), snapshots.astype(jnp.float32), (((0,), (1,)), ((), ())), preferred_element_type=jnp.float32)
    coefficients = raw * (math.sqrt(RANK) / M)
    coeff_low = coefficients.astype(jnp.bfloat16)
    recon = lax.dot_general(coeff_low.astype(jnp.float32), basis_cols.astype(jnp.float32), (((0,), (1,)), ((), ())), preferred_element_type=jnp.float32) / math.sqrt(RANK)
    residual = snapshots.astype(jnp.float32) - recon
    gram = jnp.dot(residual, residual.T, precision=lax.Precision.HIGHEST) / M
    factor = jnp.linalg.cholesky(gram)
    directions = lax.linalg.triangular_solve(factor, residual, left_side=True, lower=True).astype(jnp.bfloat16)
    return (coefficients, factor, directions)
```

```python
import functools
import math

import jax
import jax.numpy as jnp
from jax import lax
from jax.experimental import pallas as pl
from jax.experimental.pallas import tpu as pltpu
from jax.sharding import PartitionSpec as P

RANK = 1024
LANES = 128
BLOCK = 32
SUB = 8


def swap(value, axis, offset):
    count = lax.axis_size(axis)
    return lax.ppermute(value, axis, [(i, i ^ offset) for i in range(count)])


def bits(axis, first=1):
    count = lax.axis_size(axis)
    offset = first
    found = []
    while offset < count:
        found.append(offset)
        offset *= 2
    return found


def wide_split(value):
    high = value.astype(jnp.bfloat16)
    return high, (value - high.astype(jnp.float32)).astype(jnp.bfloat16)


def nt_dot(left, right):
    return lax.dot_general(left, right, (((1,), (1,)), ((), ())), preferred_element_type=jnp.float32)


def tn_dot(left, right):
    return lax.dot_general(left, right, (((0,), (0,)), ((), ())), preferred_element_type=jnp.float32)


def upper_blocks(tiles):
    return [(row, col) for row in range(tiles) for col in range(row, tiles)]


def residual_kernel(count, total_points, parity_ref, *refs):
    low_refs, basis_refs = refs[:count], refs[count : 2 * count]
    snaps_ref, high_ref, rest_ref, keep_ref, send_ref, pack_ref = refs[2 * count :]
    snaps, points = snaps_ref.shape
    chunk = 256
    for start in range(0, points, chunk):
        cols = slice(start, start + chunk)
        recon = nt_dot(low_refs[0][...], basis_refs[0][cols, :])
        for low_ref, basis_ref in zip(low_refs[1:], basis_refs[1:]):
            recon += nt_dot(low_ref[...], basis_ref[cols, :])
        residual = snaps_ref[:, cols].astype(jnp.float32) - recon * (1.0 / math.sqrt(RANK))
        high, rest = wide_split(residual)
        high_ref[:, cols] = high
        rest_ref[:, cols] = rest
    tiles = snaps // LANES
    scale = 1.0 / total_points
    for index, (row, col) in enumerate(upper_blocks(tiles)):
        rows, cols = pl.ds(row * LANES, LANES), pl.ds(col * LANES, LANES)
        block = nt_dot(high_ref[rows, :], high_ref[cols, :])
        block += nt_dot(high_ref[rows, :], rest_ref[cols, :]) + nt_dot(rest_ref[rows, :], high_ref[cols, :])
        pack_ref[pl.ds(index * LANES, LANES), :] = block * scale
    half = pack_ref.shape[0] // 2
    odd = parity_ref[0] == 1
    first, second = pack_ref[pl.ds(0, half), :], pack_ref[pl.ds(half, half), :]
    keep_ref[...] = jnp.where(odd, second, first)
    send_ref[...] = jnp.where(odd, first, second)


def row_of(tile, index):
    return jnp.broadcast_to(tile[index : index + 1, :], tile.shape)


def eliminate(panel, offset):
    groups = BLOCK // SUB
    sub_iota = lax.broadcasted_iota(jnp.int32, (SUB, LANES), 0)
    columns = [
        [jnp.broadcast_to(panel[0][g][:, offset + j : offset + j + 1], (SUB, LANES)) for g in range(groups)]
        for j in range(BLOCK)
    ]
    scales = [jnp.zeros((SUB, LANES), jnp.float32) for _ in range(groups)]
    for p in range(BLOCK):
        home, line = divmod(p, SUB)
        pivot = row_of(columns[p][home], line)
        inverse = 1.0 / pivot
        scales[home] = jnp.where(sub_iota == line, lax.rsqrt(pivot), scales[home])
        factors = {}
        for g in range(home, groups):
            value = columns[p][g] * inverse
            if g == home:
                if line == SUB - 1:
                    continue
                value = jnp.where(sub_iota > line, value, 0.0)
            factors[g] = value
        for lanes in columns[p + 1 :] + panel:
            lead = row_of(lanes[home], line)
            for g, value in factors.items():
                lanes[g] = lanes[g] - value * lead
    return [[tile * scale for tile, scale in zip(lanes, scales)] for lanes in panel]


def three_way(value):
    first = value.astype(jnp.bfloat16)
    value = value - first.astype(jnp.float32)
    second = value.astype(jnp.bfloat16)
    third = (value - second.astype(jnp.float32)).astype(jnp.bfloat16)
    return first, second, third


def factor_kernel(parity_ref, mine_ref, other_ref, high_ref, rest_ref, factor_ref, out_ref, a_ref, w_ref):
    size = factor_ref.shape[0]
    tiles = size // LANES
    half = mine_ref.shape[0]
    odd = parity_ref[0] == 1
    for index, (row, col) in enumerate(upper_blocks(tiles)):
        for start in range(0, LANES, LANES // 2):
            at = index * LANES + start
            here, there = (mine_ref, other_ref) if at < half else (other_ref, mine_ref)
            rows = pl.ds(at % half, LANES // 2)
            a_ref[pl.ds(row * LANES + start, LANES // 2), pl.ds(col * LANES, LANES)] = jnp.where(
                odd, there[rows, :], here[rows, :]
            )
    rows_iota = lax.broadcasted_iota(jnp.int32, (size, size), 0)
    cols_iota = lax.broadcasted_iota(jnp.int32, (size, size), 1)
    w_ref[...] = jnp.where(rows_iota == cols_iota, 1.0, 0.0)

    for base in range(0, size, BLOCK):
        tile, offset = divmod(base, LANES)
        a_tiles, w_tiles = range(tile, tiles), range(tile + 1)
        places = [(a_ref, t) for t in a_tiles] + [(w_ref, t) for t in w_tiles]
        panel = [
            [ref[pl.ds(base + g, SUB), pl.ds(t * LANES, LANES)] for g in range(0, BLOCK, SUB)] for ref, t in places
        ]
        panel = [jnp.concatenate(lanes, axis=0) for lanes in eliminate(panel, offset)]
        for (ref, t), value in zip(places, panel):
            ref[pl.ds(base, BLOCK), pl.ds(t * LANES, LANES)] = value
        after = base + BLOCK
        if after == size:
            break
        parts = [three_way(value) for value in panel]
        left = [jnp.concatenate([a, a, b, a, c, b], axis=0) for a, b, c in parts[: len(a_tiles)]]
        right = [jnp.concatenate([a, b, a, c, a, b], axis=0) for a, b, c in parts]
        for row_tile in a_tiles:
            skip = after - row_tile * LANES if after > row_tile * LANES else 0
            if skip == LANES:
                continue
            rows = pl.ds(row_tile * LANES + skip, LANES - skip)
            for (ref, t), value in zip(places, right):
                if ref is a_ref and t < row_tile:
                    continue
                update = tn_dot(left[row_tile - tile], value)
                lanes = pl.ds(t * LANES, LANES)
                ref[rows, lanes] = ref[rows, lanes] - update[skip:, :]

    lower = rows_iota[:LANES, :LANES] >= cols_iota[:LANES, :LANES]
    for row in range(tiles):
        for col in range(tiles):
            into = (pl.ds(row * LANES, LANES), pl.ds(col * LANES, LANES))
            if row < col:
                factor_ref[into] = jnp.zeros((LANES, LANES), jnp.float32)
                continue
            block = a_ref[pl.ds(col * LANES, LANES), pl.ds(row * LANES, LANES)].T
            factor_ref[into] = jnp.where(lower, block, 0.0) if row == col else block
    chunk = 256
    for row in range(tiles):
        depth = (row + 1) * LANES
        rows = pl.ds(row * LANES, LANES)
        high, rest = wide_split(w_ref[rows, pl.ds(0, depth)])
        for start in range(0, out_ref.shape[1], chunk):
            cols = pl.ds(start, chunk)
            right_high, right_rest = high_ref[pl.ds(0, depth), cols], rest_ref[pl.ds(0, depth), cols]
            value = jnp.dot(high, right_high, preferred_element_type=jnp.float32)
            value += jnp.dot(high, right_rest, preferred_element_type=jnp.float32)
            value += jnp.dot(rest, right_high, preferred_element_type=jnp.float32)
            out_ref[rows, cols] = value.astype(jnp.bfloat16)


def vmem_call(kernel, outs, scratch, flops):
    vmem = pl.BlockSpec(memory_space=pltpu.VMEM)
    smem = pl.BlockSpec(memory_space=pltpu.SMEM)

    def run(scalar, *args):
        size = sum(math.prod(x.shape) * x.dtype.itemsize for x in (*args, *outs))
        return pl.pallas_call(
            kernel,
            out_shape=outs,
            in_specs=[smem] + [vmem] * len(args),
            out_specs=[vmem] * len(outs),
            scratch_shapes=scratch,
            cost_estimate=pl.CostEstimate(flops=flops, bytes_accessed=size, transcendentals=0),
        )(scalar, *args)

    return run


def shards(basis_cols, snapshots):
    snaps, row_points = snapshots.shape
    modes = basis_cols.shape[1]
    row_index, column_index = lax.axis_index("rows"), lax.axis_index("cols")
    column_count = lax.axis_size("cols")
    total_points = row_points * lax.axis_size("rows")
    points = row_points // column_count
    row_odd, column_odd = row_index % 2, column_index % 2

    def slab(column):
        return lax.dynamic_slice_in_dim(basis_cols, column * points, points, 0)

    own_basis = slab(column_index)
    others = [swap(slab(column_index ^ offset), "cols", offset) for offset in range(1, column_count)]
    own_snaps = lax.dynamic_slice_in_dim(snapshots, column_index * points, points, 1)

    raw = lax.dot_general(snapshots, basis_cols, (((1,), (0,)), ((), ())), preferred_element_type=jnp.float32)
    half = snaps // 2
    sent = lax.dynamic_slice_in_dim(raw, (1 - row_odd) * half, half, 0)
    kept = lax.dynamic_slice_in_dim(raw, row_odd * half, half, 0)
    kept = kept + swap(sent, "rows", 1)
    for offset in bits("rows", 2):
        kept = kept + swap(kept, "rows", offset)
    low = (kept * (math.sqrt(RANK) / total_points)).astype(jnp.bfloat16)
    other = swap(low, "rows", 1)
    low = jnp.where(row_odd == 1, jnp.concatenate([other, low], 0), jnp.concatenate([low, other], 0))
    lows = {0: low}
    for offset in reversed(bits("cols")):
        lows.update({key ^ offset: swap(value, "cols", offset) for key, value in list(lows.items())})
    coefficients = low.astype(jnp.float32).T

    packed = len(upper_blocks(snaps // LANES)) * LANES
    part = jax.ShapeDtypeStruct((packed // 2, LANES), jnp.float32)
    wide = jax.ShapeDtypeStruct((snaps, points), jnp.bfloat16)
    odd = column_odd.astype(jnp.int32).reshape(1)
    high, rest, keep, send = vmem_call(
        functools.partial(residual_kernel, column_count, total_points),
        (wide, wide, part, part),
        [pltpu.VMEM((packed, LANES), jnp.float32)],
        2 * snaps * points * (modes * column_count + 3 * snaps),
    )(odd, *[lows[offset] for offset in range(column_count)], own_basis, *others, own_snaps)
    keep = keep + swap(send, "cols", 1)
    for axis, first in (("cols", 2), ("rows", 1)):
        for offset in bits(axis, first):
            keep = keep + swap(keep, axis, offset)
    rest_of_gram = swap(keep, "cols", 1)
    factor, directions = vmem_call(
        factor_kernel,
        (jax.ShapeDtypeStruct((snaps, snaps), jnp.float32), wide),
        [pltpu.VMEM((snaps, snaps), jnp.float32)] * 2,
        6 * snaps * snaps * points,
    )(odd, keep, rest_of_gram, high, rest)
    return (coefficients, factor, directions)


def solution(mesh):
    placed = (P("rows", "cols"), P(None, "rows"))
    return jax.shard_map(
        shards,
        mesh=mesh,
        in_specs=placed,
        out_specs=(P("cols", None), P(), P(None, ("rows", "cols"))),
        check_vma=False,
    )
```

```python
import functools
import math

import jax
import jax.numpy as jnp
from jax import lax
from jax.experimental import pallas as pl
from jax.experimental.pallas import tpu as pltpu
from jax.sharding import PartitionSpec as P


RANK = 1024
LANES = 128
BLOCK = 32
SUB = 8


def swap(value, masks):
    count = lax.axis_size("rows") * lax.axis_size("cols")
    return lax.ppermute(value, ("rows", "cols"), [(i, i ^ masks[i % 2]) for i in range(count)])


def bits(count, step=1):
    found = []
    while count > 1:
        found.append(step)
        step, count = 2 * step, count // 2
    return found


def wide_split(value):
    high = value.astype(jnp.bfloat16)
    return high, (value - high.astype(jnp.float32)).astype(jnp.bfloat16)


def nt_dot(left, right):
    return lax.dot_general(left, right, (((1,), (1,)), ((), ())), preferred_element_type=jnp.float32)


def tn_dot(left, right):
    return lax.dot_general(left, right, (((0,), (0,)), ((), ())), preferred_element_type=jnp.float32)


def project_kernel(place_ref, basis_ref, snaps_ref, keep_ref, send_ref, *refs):
    count = (len(refs) - 2) // 2
    slab_refs, part_refs, basis_sem, snaps_sem = refs[:count], refs[count : 2 * count], refs[-2], refs[-1]
    points = slab_refs[0].shape[0]
    copies = []
    for offset in range(count):
        start = pl.multiple_of((place_ref[0] ^ offset) * points, points)
        span = pl.ds(start, points)
        copies.append(
            (
                pltpu.make_async_copy(basis_ref.at[span, :], slab_refs[offset], basis_sem.at[offset]),
                pltpu.make_async_copy(snaps_ref.at[:, span], part_refs[offset], snaps_sem.at[offset]),
            )
        )
    for pair in copies:
        for copy in pair:
            copy.start()
    total = None
    for offset in range(count):
        for copy in copies[offset]:
            copy.wait()
        value = jnp.dot(part_refs[offset][...], slab_refs[offset][...], preferred_element_type=jnp.float32)
        total = value if total is None else total + value
    half = total.shape[0] // 2
    odd = place_ref[1] == 1
    first, second = total[:half, :], total[half:, :]
    keep_ref[...] = jnp.where(odd, second, first)
    send_ref[...] = jnp.where(odd, first, second)


def recon_kernel(place_ref, *refs):
    count = (len(refs) - 1) // 2
    points = refs[count].shape[0]
    chunk = 256
    for start in range(0, points, chunk):
        cols = slice(start, start + chunk)
        recon = nt_dot(refs[0][...], refs[count][cols, :])
        for low_ref, basis_ref in zip(refs[1:count], refs[count + 1 : -1]):
            recon += nt_dot(low_ref[...], basis_ref[cols, :])
        refs[-1][:, cols] = recon


def packed_rows(tiles):
    return tiles // 2 * (LANES + 2 * SUB) + tiles * (tiles - 1) // 2 * LANES


def pack_layout(tiles):
    at, pairs, blocks = 0, [], []
    for first in range(0, tiles, 2):
        pairs.append((first, at, at + LANES))
        at += LANES + 2 * SUB
    for row in range(tiles):
        for col in range(row + 1, tiles):
            blocks.append((row, col, at))
            at += LANES
    return pairs, blocks


def square_iota(dim):
    return lax.broadcasted_iota(jnp.int32, (LANES, LANES), dim)


def residual_kernel(total_points, place_ref, *refs):
    count = (len(refs) - 7) // 2
    low_refs, basis_refs = refs[:count], refs[count : 2 * count]
    begun_ref, snaps_ref, high_ref, rest_ref, keep_ref, send_ref, pack_ref = refs[2 * count :]
    snaps, points = snaps_ref.shape
    chunk = 256
    for start in range(0, points, chunk):
        cols = slice(start, start + chunk)
        recon = begun_ref[:, cols]
        for low_ref, basis_ref in zip(low_refs, basis_refs):
            recon += nt_dot(low_ref[...], basis_ref[cols, :])
        residual = snaps_ref[:, cols].astype(jnp.float32) - recon * (1.0 / math.sqrt(RANK))
        high, rest = wide_split(residual)
        high_ref[:, cols] = high
        rest_ref[:, cols] = rest
    scale = 1.0 / total_points

    def block(row, col):
        rows, cols = pl.ds(row * LANES, LANES), pl.ds(col * LANES, LANES)
        value = nt_dot(high_ref[rows, :], high_ref[cols, :])
        value += nt_dot(high_ref[rows, :], rest_ref[cols, :]) + nt_dot(rest_ref[rows, :], high_ref[cols, :])
        return value * scale

    pairs, blocks = pack_layout(snaps // LANES)
    down, across = square_iota(0), square_iota(1)
    for first, at, line in pairs:
        upper, lower = block(first, first), block(first + 1, first + 1)
        pack_ref[pl.ds(at, LANES), :] = jnp.where(down <= across, upper, lower)
        diagonal = jnp.sum(jnp.where(down == across, lower, 0.0), axis=0, keepdims=True)
        pack_ref[pl.ds(line, 2 * SUB), :] = jnp.broadcast_to(diagonal, (2 * SUB, LANES))
    for row, col, at in blocks:
        pack_ref[pl.ds(at, LANES), :] = block(row, col)
    half = pack_ref.shape[0] // 2
    odd = place_ref[0] % 2 == 1
    first, second = pack_ref[pl.ds(0, half), :], pack_ref[pl.ds(half, half), :]
    keep_ref[...] = jnp.where(odd, second, first)
    send_ref[...] = jnp.where(odd, first, second)


def row_of(tile, index):
    return jnp.broadcast_to(tile[index : index + 1, :], tile.shape)


def eliminate(panel, offset):
    groups = BLOCK // SUB
    sub_iota = lax.broadcasted_iota(jnp.int32, (SUB, LANES), 0)
    columns = [
        [jnp.broadcast_to(panel[0][g][:, offset + j : offset + j + 1], (SUB, LANES)) for g in range(groups)]
        for j in range(BLOCK)
    ]
    scales = [jnp.zeros((SUB, LANES), jnp.float32) for _ in range(groups)]
    for p in range(BLOCK):
        home, line = divmod(p, SUB)
        pivot = row_of(columns[p][home], line)
        inverse = 1.0 / pivot
        scales[home] = jnp.where(sub_iota == line, lax.rsqrt(pivot), scales[home])
        factors = {}
        for g in range(home, groups):
            value = columns[p][g] * inverse
            if g == home:
                if line == SUB - 1:
                    continue
                value = jnp.where(sub_iota > line, value, 0.0)
            factors[g] = value
        for lanes in columns[p + 1 :] + panel:
            lead = row_of(lanes[home], line)
            for g, value in factors.items():
                lanes[g] = lanes[g] - value * lead
    return [[tile * scale for tile, scale in zip(lanes, scales)] for lanes in panel]


def three_way(value):
    first = value.astype(jnp.bfloat16)
    value = value - first.astype(jnp.float32)
    second = value.astype(jnp.bfloat16)
    third = (value - second.astype(jnp.float32)).astype(jnp.bfloat16)
    return first, second, third


def factor_kernel(place_ref, mine_ref, other_ref, high_ref, rest_ref, factor_ref, out_ref, a_ref, w_ref, pack_ref):
    size = factor_ref.shape[0]
    tiles = size // LANES
    half = mine_ref.shape[0]
    odd = place_ref[0] % 2 == 1
    pack_ref[pl.ds(0, half), :] = jnp.where(odd, other_ref[...], mine_ref[...])
    pack_ref[pl.ds(half, half), :] = jnp.where(odd, mine_ref[...], other_ref[...])
    pairs, blocks = pack_layout(tiles)
    down, across = square_iota(0), square_iota(1)

    def square(tile):
        return pl.ds(tile * LANES, LANES), pl.ds(tile * LANES, LANES)

    for first, at, line in pairs:
        folded = pack_ref[pl.ds(at, LANES), :]
        turned = folded.T
        a_ref[square(first)] = jnp.where(down <= across, folded, turned)
        diagonal = jnp.broadcast_to(pack_ref[pl.ds(line, 1), :], (LANES, LANES))
        value = jnp.where(down > across, folded, turned)
        a_ref[square(first + 1)] = jnp.where(down == across, diagonal, value)
    for row, col, at in blocks:
        a_ref[pl.ds(row * LANES, LANES), pl.ds(col * LANES, LANES)] = pack_ref[pl.ds(at, LANES), :]
    rows_iota = lax.broadcasted_iota(jnp.int32, (size, size), 0)
    cols_iota = lax.broadcasted_iota(jnp.int32, (size, size), 1)
    w_ref[...] = jnp.where(rows_iota == cols_iota, 1.0, 0.0)

    for base in range(0, size, BLOCK):
        tile, offset = divmod(base, LANES)
        a_tiles, w_tiles = range(tile, tiles), range(tile + 1)
        places = [(a_ref, t) for t in a_tiles] + [(w_ref, t) for t in w_tiles]
        panel = [
            [ref[pl.ds(base + g, SUB), pl.ds(t * LANES, LANES)] for g in range(0, BLOCK, SUB)] for ref, t in places
        ]
        panel = [jnp.concatenate(lanes, axis=0) for lanes in eliminate(panel, offset)]
        for (ref, t), value in zip(places, panel):
            ref[pl.ds(base, BLOCK), pl.ds(t * LANES, LANES)] = value
        after = base + BLOCK
        if after == size:
            break
        parts = [three_way(value) for value in panel]
        left = [jnp.concatenate([a, a, b, a, c, b], axis=0) for a, b, c in parts[: len(a_tiles)]]
        right = [jnp.concatenate([a, b, a, c, a, b], axis=0) for a, b, c in parts]
        for row_tile in a_tiles:
            skip = after - row_tile * LANES if after > row_tile * LANES else 0
            if skip == LANES:
                continue
            rows = pl.ds(row_tile * LANES + skip, LANES - skip)
            for (ref, t), value in zip(places, right):
                if ref is a_ref and t < row_tile:
                    continue
                update = tn_dot(left[row_tile - tile], value)
                lanes = pl.ds(t * LANES, LANES)
                ref[rows, lanes] = ref[rows, lanes] - update[skip:, :]

    lower = rows_iota[:LANES, :LANES] >= cols_iota[:LANES, :LANES]
    for row in range(tiles):
        for col in range(tiles):
            into = (pl.ds(row * LANES, LANES), pl.ds(col * LANES, LANES))
            if row < col:
                factor_ref[into] = jnp.zeros((LANES, LANES), jnp.float32)
                continue
            block = a_ref[pl.ds(col * LANES, LANES), pl.ds(row * LANES, LANES)].T
            factor_ref[into] = jnp.where(lower, block, 0.0) if row == col else block
    chunk = 256
    for row in range(tiles):
        depth = (row + 1) * LANES
        rows = pl.ds(row * LANES, LANES)
        high, rest = wide_split(w_ref[rows, pl.ds(0, depth)])
        for start in range(0, out_ref.shape[1], chunk):
            cols = pl.ds(start, chunk)
            right_high, right_rest = high_ref[pl.ds(0, depth), cols], rest_ref[pl.ds(0, depth), cols]
            value = jnp.dot(high, right_high, preferred_element_type=jnp.float32)
            value += jnp.dot(high, right_rest, preferred_element_type=jnp.float32)
            value += jnp.dot(rest, right_high, preferred_element_type=jnp.float32)
            out_ref[rows, cols] = value.astype(jnp.bfloat16)


def call(kernel, outs, scratch, flops, grant, whole=0):
    vmem = pl.BlockSpec(memory_space=pltpu.VMEM)
    smem = pl.BlockSpec(memory_space=pltpu.SMEM)
    anywhere = pl.BlockSpec(memory_space=pl.ANY)

    def run(scalar, *args):
        size = sum(math.prod(x.shape) * x.dtype.itemsize for x in (*args, *outs))
        return pl.pallas_call(
            kernel,
            out_shape=outs,
            in_specs=[smem] + [anywhere] * whole + [vmem] * (len(args) - whole),
            out_specs=[vmem] * len(outs),
            scratch_shapes=scratch,
            compiler_params=pltpu.CompilerParams(vmem_limit_bytes=grant << 20),
            cost_estimate=pl.CostEstimate(flops=flops, bytes_accessed=size, transcendentals=0),
        )(scalar, *args)

    return run


def shape(dtype, *dims):
    return jax.ShapeDtypeStruct(dims, dtype)


def compute(basis_cols, snapshots):
    snaps, row_points = snapshots.shape
    modes = basis_cols.shape[1]
    row_index, column_index = lax.axis_index("rows"), lax.axis_index("cols")
    row_count, columns = lax.axis_size("rows"), lax.axis_size("cols")
    total_points = row_points * row_count
    points = row_points // columns
    half = snaps // 2
    bf16, f32 = jnp.bfloat16, jnp.float32

    row_bits = bits(row_count, columns)
    sum_steps = list(zip(row_bits, row_bits[1:] + row_bits[:1]))
    flat = row_index * columns + column_index
    odd = (flat // jnp.where(column_index % 2 == 0, sum_steps[0][0], sum_steps[0][1])) % 2
    place = jnp.stack([column_index, odd]).astype(jnp.int32)

    kept, sent, *slabs = call(
        project_kernel,
        (shape(f32, half, modes),) * 2 + (shape(bf16, points, modes),) * columns + (shape(bf16, snaps, points),),
        [pltpu.VMEM((snaps, points), bf16)] * (columns - 1)
        + [pltpu.SemaphoreType.DMA((columns,)), pltpu.SemaphoreType.DMA((columns,))],
        2 * snaps * row_points * modes,
        16,
        2,
    )(place, basis_cols, snapshots)
    own_snaps = slabs.pop()
    for offset in reversed(range(1, columns)):
        slabs[offset] = swap(slabs[offset], (offset, offset))

    arrived = swap(sent, sum_steps[0])
    kept = kept + arrived
    for step in sum_steps[1:]:
        kept = kept + swap(kept, step)
    low = (kept * (math.sqrt(RANK) / total_points)).astype(bf16)
    other = swap(low, sum_steps[0])
    low = jnp.where(odd == 1, jnp.concatenate([other, low], 0), jnp.concatenate([low, other], 0))
    coefficients = low.astype(f32).T
    lows = {0: low}
    near = swap(low, (1, 1))
    for offset in reversed(bits(columns // 2, 2)):
        lows.update({key ^ offset: swap(value, (offset, offset)) for key, value in list(lows.items())})
    lows.update({key ^ 1: near if key == 0 else swap(value, (1, 1)) for key, value in list(lows.items())})

    (begun,) = call(recon_kernel, (shape(f32, snaps, points),), [], 4 * snaps * points * modes, 8)(
        place, lows[0], lows[1], slabs[0], slabs[1]
    )
    packed = packed_rows(snaps // LANES)
    part = shape(f32, packed // 2, LANES)
    wide = shape(bf16, snaps, points)
    high, rest, keep, send = call(
        functools.partial(residual_kernel, total_points),
        (wide, wide, part, part),
        [pltpu.VMEM((packed, LANES), f32)],
        2 * snaps * points * (modes * (columns - 2) + 3 * snaps),
        16,
    )(place, *[lows[offset] for offset in range(2, columns)], *slabs[2:], begun, own_snaps)
    keep = keep + swap(send, (1, 1))
    rest_bits = bits(columns // 2, 2) + row_bits
    first_order = rest_bits[-1:] + rest_bits[:-1]
    second_order = list(first_order)
    for at in range(0, len(first_order) - 1, 2):
        second_order[at : at + 2] = reversed(first_order[at : at + 2])
    for step in zip(first_order, second_order):
        keep = keep + swap(keep, step)
    rest_of_gram = swap(keep, (1, 1))
    factor, directions = call(
        factor_kernel,
        (shape(f32, snaps, snaps), wide),
        [pltpu.VMEM((snaps, snaps), f32)] * 2 + [pltpu.VMEM((packed, LANES), f32)],
        6 * snaps * snaps * points,
        16,
    )(place, keep, rest_of_gram, high, rest)
    return (coefficients, factor, directions)


def solution(mesh):
    placed = (P("rows", "cols"), P(None, "rows"))
    return jax.shard_map(
        compute,
        mesh=mesh,
        in_specs=placed,
        out_specs=(P("cols", None), P(), P(None, ("rows", "cols"))),
        check_vma=False,
    )
```

```python
import functools
import math

import jax
import jax.numpy as jnp
from jax import lax
from jax.experimental import pallas as pl
from jax.experimental.pallas import tpu as pltpu
from jax.sharding import PartitionSpec as P


RANK = 1024
LANES = 128
BLOCK = 64
STEP = 16
SUB = 8


def swap(value, masks):
    count = lax.axis_size("rows") * lax.axis_size("cols")
    return lax.ppermute(value, ("rows", "cols"), [(i, i ^ masks[i % 2]) for i in range(count)])


def bits(count, step=1):
    found = []
    while count > 1:
        found.append(step)
        step, count = 2 * step, count // 2
    return found


def wide_split(value):
    high = value.astype(jnp.bfloat16)
    return high, (value - high.astype(jnp.float32)).astype(jnp.bfloat16)


def nt_dot(left, right):
    return lax.dot_general(left, right, (((1,), (1,)), ((), ())), preferred_element_type=jnp.float32)


def tn_dot(left, right):
    return lax.dot_general(left, right, (((0,), (0,)), ((), ())), preferred_element_type=jnp.float32)


def slab_copies(place_ref, whole_ref, into_refs, sem_ref, first, by_rows):
    copies = []
    for index, into_ref in enumerate(into_refs):
        size = into_ref.shape[0 if by_rows else 1]
        start = pl.multiple_of((place_ref[0] ^ (first + index)) * size, size)
        span = whole_ref.at[pl.ds(start, size), :] if by_rows else whole_ref.at[:, pl.ds(start, size)]
        copies.append(pltpu.make_async_copy(span, into_ref, sem_ref.at[index]))
    return copies


def slab_kernel(place_ref, basis_ref, *refs):
    copies = slab_copies(place_ref, basis_ref, refs[:-1], refs[-1], 2, True)
    for copy in copies:
        copy.start()
    for copy in copies:
        copy.wait()


def project_kernel(place_ref, basis_ref, snaps_ref, *refs):
    count = (len(refs) - 3) // 2
    far_refs = refs[: count - 2]
    keep_ref, send_ref, own_ref, near_ref = refs[count - 2 : count + 2]
    part_refs, basis_sem, snaps_sem = refs[count + 2 : -2], refs[-2], refs[-1]
    basis_copies = slab_copies(place_ref, basis_ref, (own_ref, near_ref), basis_sem, 0, True)
    snaps_copies = slab_copies(place_ref, snaps_ref, part_refs, snaps_sem, 0, False)
    for copy in snaps_copies[2:] + basis_copies + snaps_copies[:2]:
        copy.start()
    total = None
    order = list(range(2, count)) + [0, 1]
    slab_refs = (own_ref, near_ref) + tuple(far_refs)
    for offset in order:
        snaps_copies[offset].wait()
        if offset < 2:
            basis_copies[offset].wait()
        value = jnp.dot(part_refs[offset][...], slab_refs[offset][...], preferred_element_type=jnp.float32)
        total = value if total is None else total + value
    half = total.shape[0] // 2
    odd = place_ref[1] == 1
    first, second = total[:half, :], total[half:, :]
    keep_ref[...] = jnp.where(odd, second, first)
    send_ref[...] = jnp.where(odd, first, second)


def recon_kernel(place_ref, *refs):
    recon_ref, coefficients_ref = refs[-2:]
    coefficients_ref[...] = refs[0][...].astype(jnp.float32).T
    chunk = 256
    for start in range(0, recon_ref.shape[1], chunk):
        cols = slice(start, start + chunk)
        recon_ref[:, cols] = nt_dot(refs[0][...], refs[2][cols, :]) + nt_dot(refs[1][...], refs[3][cols, :])


def packed_rows(tiles):
    return tiles // 2 * (LANES + 2 * SUB) + tiles * (tiles - 1) // 2 * LANES


def pack_layout(tiles):
    at, pairs, blocks = 0, [], []
    for first in range(0, tiles, 2):
        pairs.append((first, at, at + LANES))
        at += LANES + 2 * SUB
    for row in range(tiles):
        for col in range(row + 1, tiles):
            blocks.append((row, col, at))
            at += LANES
    return pairs, blocks


def square_iota(dim):
    return lax.broadcasted_iota(jnp.int32, (LANES, LANES), dim)


def residual_kernel(total_points, place_ref, *refs):
    count = (len(refs) - 7) // 2
    low_refs, basis_refs = refs[:count], refs[count : 2 * count]
    begun_ref, snaps_ref, high_ref, rest_ref, keep_ref, send_ref, pack_ref = refs[2 * count :]
    snaps, points = snaps_ref.shape
    chunk = 256
    for start in range(0, points, chunk):
        cols = slice(start, start + chunk)
        recon = begun_ref[:, cols]
        for low_ref, basis_ref in zip(low_refs, basis_refs):
            recon += nt_dot(low_ref[...], basis_ref[cols, :])
        residual = snaps_ref[:, cols].astype(jnp.float32) - recon * (1.0 / math.sqrt(RANK))
        high, rest = wide_split(residual)
        high_ref[:, cols] = high
        rest_ref[:, cols] = rest
    scale = 1.0 / total_points

    def block(row, col):
        rows, cols = pl.ds(row * LANES, LANES), pl.ds(col * LANES, LANES)
        value = nt_dot(high_ref[rows, :], high_ref[cols, :])
        value += nt_dot(high_ref[rows, :], rest_ref[cols, :]) + nt_dot(rest_ref[rows, :], high_ref[cols, :])
        return value * scale

    pairs, blocks = pack_layout(snaps // LANES)
    down, across = square_iota(0), square_iota(1)
    for first, at, line in pairs:
        upper, lower = block(first, first), block(first + 1, first + 1)
        pack_ref[pl.ds(at, LANES), :] = jnp.where(down <= across, upper, lower)
        diagonal = jnp.sum(jnp.where(down == across, lower, 0.0), axis=0, keepdims=True)
        pack_ref[pl.ds(line, 2 * SUB), :] = jnp.broadcast_to(diagonal, (2 * SUB, LANES))
    for row, col, at in blocks:
        pack_ref[pl.ds(at, LANES), :] = block(row, col)
    half = pack_ref.shape[0] // 2
    odd = place_ref[0] % 2 == 1
    first, second = pack_ref[pl.ds(0, half), :], pack_ref[pl.ds(half, half), :]
    keep_ref[...] = jnp.where(odd, second, first)
    send_ref[...] = jnp.where(odd, first, second)


def row_of(tile, index):
    return jnp.broadcast_to(tile[index : index + 1, :], tile.shape)


def eliminate(panel, offset):
    groups = BLOCK // SUB
    sub_iota = lax.broadcasted_iota(jnp.int32, (SUB, LANES), 0)
    scales = [jnp.zeros((SUB, LANES), jnp.float32) for _ in range(groups)]
    for begin in range(0, BLOCK, STEP):
        columns = [
            [
                jnp.broadcast_to(panel[0][g][:, offset + j : offset + j + 1], (SUB, LANES))
                if g >= begin // SUB
                else None
                for g in range(groups)
            ]
            for j in range(begin, begin + STEP)
        ]
        for p in range(begin, begin + STEP):
            home, line = divmod(p, SUB)
            column = columns[p - begin]
            pivot = row_of(column[home], line)
            inverse = 1.0 / pivot
            scales[home] = jnp.where(sub_iota == line, lax.rsqrt(pivot), scales[home])
            factors = {}
            for g in range(home, groups):
                value = column[g] * inverse
                if g == home:
                    if line == SUB - 1:
                        continue
                    value = jnp.where(sub_iota > line, value, 0.0)
                factors[g] = value
            for lanes in columns[p - begin + 1 :] + panel:
                lead = row_of(lanes[home], line)
                for g, value in factors.items():
                    lanes[g] = lanes[g] - value * lead
    return [[tile * scale for tile, scale in zip(lanes, scales)] for lanes in panel]


def factor_kernel(place_ref, mine_ref, other_ref, high_ref, rest_ref, factor_ref, out_ref, a_ref, w_ref, pack_ref):
    size = factor_ref.shape[0]
    tiles = size // LANES
    half = mine_ref.shape[0]
    odd = place_ref[0] % 2 == 1
    pack_ref[pl.ds(0, half), :] = jnp.where(odd, other_ref[...], mine_ref[...])
    pack_ref[pl.ds(half, half), :] = jnp.where(odd, mine_ref[...], other_ref[...])
    pairs, blocks = pack_layout(tiles)
    down, across = square_iota(0), square_iota(1)

    def square(tile):
        return pl.ds(tile * LANES, LANES), pl.ds(tile * LANES, LANES)

    for first, at, line in pairs:
        folded = pack_ref[pl.ds(at, LANES), :]
        turned = folded.T
        a_ref[square(first)] = jnp.where(down <= across, folded, turned)
        diagonal = jnp.broadcast_to(pack_ref[pl.ds(line, 1), :], (LANES, LANES))
        value = jnp.where(down > across, folded, turned)
        a_ref[square(first + 1)] = jnp.where(down == across, diagonal, value)
    for row, col, at in blocks:
        a_ref[pl.ds(row * LANES, LANES), pl.ds(col * LANES, LANES)] = pack_ref[pl.ds(at, LANES), :]
    rows_iota = lax.broadcasted_iota(jnp.int32, (size, size), 0)
    cols_iota = lax.broadcasted_iota(jnp.int32, (size, size), 1)
    w_ref[...] = jnp.where(rows_iota == cols_iota, 1.0, 0.0)

    for base in range(0, size, BLOCK):
        tile, offset = divmod(base, LANES)
        a_tiles, w_tiles = range(tile, tiles), range(tile + 1)
        places = [(a_ref, t) for t in a_tiles] + [(w_ref, t) for t in w_tiles]
        panel = [
            [ref[pl.ds(base + g, SUB), pl.ds(t * LANES, LANES)] for g in range(0, BLOCK, SUB)] for ref, t in places
        ]
        panel = [jnp.concatenate(lanes, axis=0) for lanes in eliminate(panel, offset)]
        for (ref, t), value in zip(places, panel):
            ref[pl.ds(base, BLOCK), pl.ds(t * LANES, LANES)] = value
        after = base + BLOCK
        if after == size:
            break
        parts = [wide_split(value) for value in panel]
        left = [jnp.concatenate([a, a, b], axis=0) for a, b in parts[: len(a_tiles)]]
        right = [jnp.concatenate([a, b, a], axis=0) for a, b in parts]
        for row_tile in a_tiles:
            skip = after - row_tile * LANES if after > row_tile * LANES else 0
            if skip == LANES:
                continue
            rows = pl.ds(row_tile * LANES + skip, LANES - skip)
            for (ref, t), value in zip(places, right):
                if ref is a_ref and t < row_tile:
                    continue
                update = tn_dot(left[row_tile - tile], value)
                lanes = pl.ds(t * LANES, LANES)
                ref[rows, lanes] = ref[rows, lanes] - update[skip:, :]

    lower = rows_iota[:LANES, :LANES] >= cols_iota[:LANES, :LANES]
    for row in range(tiles):
        for col in range(tiles):
            into = (pl.ds(row * LANES, LANES), pl.ds(col * LANES, LANES))
            if row < col:
                factor_ref[into] = jnp.zeros((LANES, LANES), jnp.float32)
                continue
            block = a_ref[pl.ds(col * LANES, LANES), pl.ds(row * LANES, LANES)].T
            factor_ref[into] = jnp.where(lower, block, 0.0) if row == col else block
    chunk = 256
    for row in range(tiles):
        depth = (row + 1) * LANES
        rows = pl.ds(row * LANES, LANES)
        high, rest = wide_split(w_ref[rows, pl.ds(0, depth)])
        for start in range(0, out_ref.shape[1], chunk):
            cols = pl.ds(start, chunk)
            right_high, right_rest = high_ref[pl.ds(0, depth), cols], rest_ref[pl.ds(0, depth), cols]
            value = jnp.dot(high, right_high, preferred_element_type=jnp.float32)
            value += jnp.dot(high, right_rest, preferred_element_type=jnp.float32)
            value += jnp.dot(rest, right_high, preferred_element_type=jnp.float32)
            out_ref[rows, cols] = value.astype(jnp.bfloat16)


def call(kernel, outs, scratch, flops, grant, whole=0):
    vmem = pl.BlockSpec(memory_space=pltpu.VMEM)
    smem = pl.BlockSpec(memory_space=pltpu.SMEM)
    hbm = pl.BlockSpec(memory_space=pltpu.HBM)

    def run(scalar, *args):
        size = sum(math.prod(x.shape) * x.dtype.itemsize for x in (*args, *outs))
        args = [pltpu.with_memory_space_constraint(x, pltpu.HBM) for x in args[:whole]] + list(args[whole:])
        return pl.pallas_call(
            kernel,
            out_shape=outs,
            in_specs=[smem] + [hbm] * whole + [vmem] * (len(args) - whole),
            out_specs=[vmem] * len(outs),
            scratch_shapes=scratch,
            compiler_params=pltpu.CompilerParams(vmem_limit_bytes=grant << 20),
            cost_estimate=pl.CostEstimate(flops=flops, bytes_accessed=size, transcendentals=0),
        )(scalar, *args)

    return run


def shape(dtype, *dims):
    return jax.ShapeDtypeStruct(dims, dtype)


def compute(basis_cols, snapshots):
    snaps, row_points = snapshots.shape
    modes = basis_cols.shape[1]
    row_index, column_index = lax.axis_index("rows"), lax.axis_index("cols")
    row_count, columns = lax.axis_size("rows"), lax.axis_size("cols")
    total_points = row_points * row_count
    points = row_points // columns
    half = snaps // 2
    bf16, f32 = jnp.bfloat16, jnp.float32

    row_bits = bits(row_count, columns)
    sum_steps = list(zip(row_bits, row_bits[1:] + row_bits[:1]))
    flat = row_index * columns + column_index
    odd = (flat // jnp.where(column_index % 2 == 0, sum_steps[0][0], sum_steps[0][1])) % 2
    place = jnp.stack([column_index, odd]).astype(jnp.int32)

    slab = shape(bf16, points, modes)
    semaphores = pltpu.SemaphoreType.DMA((columns,))
    far_slabs = call(slab_kernel, (slab,) * (columns - 2), [semaphores], 0, 8, 1)(place, basis_cols)
    arrived_slabs = [swap(far_slabs[at], (2 + at,) * 2) for at in range(columns - 2)]
    part = shape(f32, half, modes)
    kept, sent, own_slab, near_slab, own_snaps = call(
        project_kernel,
        (part, part, slab, slab, shape(bf16, snaps, points)),
        [pltpu.VMEM((snaps, points), bf16)] * (columns - 1) + [semaphores, semaphores],
        2 * snaps * row_points * modes,
        12,
        2,
    )(place, basis_cols, snapshots, *far_slabs)
    arrived = swap(sent, sum_steps[0])
    near_slab = swap(near_slab, (1, 1))
    kept = kept + arrived
    for step in sum_steps[1:]:
        kept = kept + swap(kept, step)
    low = (kept * (math.sqrt(RANK) / total_points)).astype(bf16)
    lows = {}
    for offset in range(0, columns, 2):
        own = swap(low, (offset, offset)) if offset else low
        other = swap(low, tuple(mask ^ offset for mask in sum_steps[0]))
        lows[offset] = jnp.concatenate([jnp.where(odd == 1, other, own), jnp.where(odd == 1, own, other)], 0)
        lows[offset + 1] = swap(lows[offset], (1, 1))

    begun, coefficients = call(
        recon_kernel, (shape(f32, snaps, points), shape(f32, modes, snaps)), [], 4 * snaps * points * modes, 8
    )(place, lows[0], lows[1], own_slab, near_slab)
    packed = packed_rows(snaps // LANES)
    part = shape(f32, packed // 2, LANES)
    wide = shape(bf16, snaps, points)
    high, rest, keep, send = call(
        functools.partial(residual_kernel, total_points),
        (wide, wide, part, part),
        [pltpu.VMEM((packed, LANES), f32)],
        2 * snaps * points * (modes * (columns - 2) + 3 * snaps),
        16,
    )(place, *[lows[offset] for offset in range(2, columns)], *arrived_slabs, begun, own_snaps)
    keep = keep + swap(send, (1, 1))
    rest_bits = bits(columns // 2, 2) + row_bits
    first_order = rest_bits[-1:] + rest_bits[:-1]
    second_order = list(first_order)
    for at in range(0, len(first_order) - 1, 2):
        second_order[at : at + 2] = reversed(first_order[at : at + 2])
    for step in zip(first_order, second_order):
        keep = keep + swap(keep, step)
    rest_of_gram = swap(keep, (1, 1))
    factor, directions = call(
        factor_kernel,
        (shape(f32, snaps, snaps), wide),
        [pltpu.VMEM((snaps, snaps), f32)] * 2 + [pltpu.VMEM((packed, LANES), f32)],
        6 * snaps * snaps * points,
        16,
    )(place, keep, rest_of_gram, high, rest)
    return (coefficients, factor, directions)


def solution(mesh):
    placed = (P("rows", "cols"), P(None, "rows"))
    return jax.shard_map(
        compute,
        mesh=mesh,
        in_specs=placed,
        out_specs=(P("cols", None), P(), P(None, ("rows", "cols"))),
        check_vma=False,
    )
```

```python
import functools
import math

import jax
import jax.numpy as jnp
from jax import lax
from jax.experimental import pallas as pl
from jax.experimental.pallas import tpu as pltpu
from jax.sharding import PartitionSpec as P


RANK = 1024
LANES = 128
BLOCK = 64
STEP = 16
SUB = 8


def swap(value, masks):
    count = lax.axis_size("rows") * lax.axis_size("cols")
    return lax.ppermute(value, ("rows", "cols"), [(i, i ^ masks[i % 2]) for i in range(count)])


def bits(count, step=1):
    found = []
    while count > 1:
        found.append(step)
        step, count = 2 * step, count // 2
    return found


def exchange_rounds(masks):
    rounds = [(masks[at], masks[at + 1] if at + 1 < len(masks) else 0) for at in range(0, len(masks), 2)]
    paired = [pair for pair in rounds if pair[1]]
    single = [pair for pair in rounds if not pair[1]]
    return paired + single, paired[::-1] + single


def wide_split(value):
    high = value.astype(jnp.bfloat16)
    return high, (value - high.astype(jnp.float32)).astype(jnp.bfloat16)


def nt_dot(left, right):
    return lax.dot_general(left, right, (((1,), (1,)), ((), ())), preferred_element_type=jnp.float32)


def tn_dot(left, right):
    return lax.dot_general(left, right, (((0,), (0,)), ((), ())), preferred_element_type=jnp.float32)


def project_kernel(place_ref, basis_ref, snaps_ref, keep_ref, send_ref, *refs):
    count = (len(refs) - 2) // 2
    slab_refs, part_refs, basis_sem, snaps_sem = refs[:count], refs[count : 2 * count], refs[-2], refs[-1]
    points = slab_refs[0].shape[0]
    copies = []
    for offset in range(count):
        start = pl.multiple_of((place_ref[0] ^ offset) * points, points)
        span = pl.ds(start, points)
        copies.append(
            (
                pltpu.make_async_copy(basis_ref.at[span, :], slab_refs[offset], basis_sem.at[offset]),
                pltpu.make_async_copy(snaps_ref.at[:, span], part_refs[offset], snaps_sem.at[offset]),
            )
        )
    for pair in copies:
        for copy in pair:
            copy.start()
    total = None
    for offset in range(count):
        for copy in copies[offset]:
            copy.wait()
        value = jnp.dot(part_refs[offset][...], slab_refs[offset][...], preferred_element_type=jnp.float32)
        total = value if total is None else total + value
    half = total.shape[0] // 2
    odd = place_ref[1] == 1
    first, second = total[:half, :], total[half:, :]
    keep_ref[...] = jnp.where(odd, second, first)
    send_ref[...] = jnp.where(odd, first, second)


def recon_kernel(place_ref, *refs):
    recon_ref, coefficients_ref = refs[-2:]
    coefficients_ref[...] = refs[0][...].astype(jnp.float32).T
    chunk = 256
    for start in range(0, recon_ref.shape[1], chunk):
        cols = slice(start, start + chunk)
        recon_ref[:, cols] = nt_dot(refs[0][...], refs[2][cols, :]) + nt_dot(refs[1][...], refs[3][cols, :])


def packed_rows(tiles):
    return tiles // 2 * (LANES + 2 * SUB) + tiles * (tiles - 1) // 2 * LANES


def pack_layout(tiles):
    at, pairs, blocks = 0, [], []
    for first in range(0, tiles, 2):
        pairs.append((first, at, at + LANES))
        at += LANES + 2 * SUB
    for row in range(tiles):
        for col in range(row + 1, tiles):
            blocks.append((row, col, at))
            at += LANES
    return pairs, blocks


def square_iota(dim):
    return lax.broadcasted_iota(jnp.int32, (LANES, LANES), dim)


def residual_kernel(total_points, place_ref, *refs):
    count = (len(refs) - 7) // 2
    low_refs, basis_refs = refs[:count], refs[count : 2 * count]
    begun_ref, snaps_ref, high_ref, rest_ref, keep_ref, send_ref, pack_ref = refs[2 * count :]
    snaps, points = snaps_ref.shape
    chunk = 256
    for start in range(0, points, chunk):
        cols = slice(start, start + chunk)
        recon = begun_ref[:, cols]
        for low_ref, basis_ref in zip(low_refs, basis_refs):
            recon += nt_dot(low_ref[...], basis_ref[cols, :])
        residual = snaps_ref[:, cols].astype(jnp.float32) - recon * (1.0 / math.sqrt(RANK))
        high, rest = wide_split(residual)
        high_ref[:, cols] = high
        rest_ref[:, cols] = rest
    scale = 1.0 / total_points

    def block(row, col):
        rows, cols = pl.ds(row * LANES, LANES), pl.ds(col * LANES, LANES)
        value = nt_dot(high_ref[rows, :], high_ref[cols, :])
        value += nt_dot(high_ref[rows, :], rest_ref[cols, :]) + nt_dot(rest_ref[rows, :], high_ref[cols, :])
        return value * scale

    pairs, blocks = pack_layout(snaps // LANES)
    down, across = square_iota(0), square_iota(1)
    for first, at, line in pairs:
        upper, lower = block(first, first), block(first + 1, first + 1)
        pack_ref[pl.ds(at, LANES), :] = jnp.where(down <= across, upper, lower)
        diagonal = jnp.sum(jnp.where(down == across, lower, 0.0), axis=0, keepdims=True)
        pack_ref[pl.ds(line, 2 * SUB), :] = jnp.broadcast_to(diagonal, (2 * SUB, LANES))
    for row, col, at in blocks:
        pack_ref[pl.ds(at, LANES), :] = block(row, col)
    half = pack_ref.shape[0] // 2
    odd = place_ref[0] % 2 == 1
    first, second = pack_ref[pl.ds(0, half), :], pack_ref[pl.ds(half, half), :]
    keep_ref[...] = jnp.where(odd, second, first)
    send_ref[...] = jnp.where(odd, first, second)


def row_of(tile, index):
    return jnp.broadcast_to(tile[index : index + 1, :], tile.shape)


def eliminate(panel, offset):
    groups = BLOCK // SUB
    sub_iota = lax.broadcasted_iota(jnp.int32, (SUB, LANES), 0)
    scales = [jnp.zeros((SUB, LANES), jnp.float32) for _ in range(groups)]
    for begin in range(0, BLOCK, STEP):
        columns = [
            [
                jnp.broadcast_to(panel[0][g][:, offset + j : offset + j + 1], (SUB, LANES))
                if g >= begin // SUB
                else None
                for g in range(groups)
            ]
            for j in range(begin, begin + STEP)
        ]
        for p in range(begin, begin + STEP):
            home, line = divmod(p, SUB)
            column = columns[p - begin]
            pivot = row_of(column[home], line)
            inverse = 1.0 / pivot
            scales[home] = jnp.where(sub_iota == line, lax.rsqrt(pivot), scales[home])
            factors = {}
            for g in range(home, groups):
                value = column[g] * inverse
                if g == home:
                    if line == SUB - 1:
                        continue
                    value = jnp.where(sub_iota > line, value, 0.0)
                factors[g] = value
            for lanes in columns[p - begin + 1 :] + panel:
                lead = row_of(lanes[home], line)
                for g, value in factors.items():
                    lanes[g] = lanes[g] - value * lead
    return [[tile * scale for tile, scale in zip(lanes, scales)] for lanes in panel]


def factor_kernel(place_ref, mine_ref, other_ref, high_ref, rest_ref, factor_ref, out_ref, a_ref, w_ref, pack_ref):
    size = factor_ref.shape[0]
    tiles = size // LANES
    half = mine_ref.shape[0]
    odd = place_ref[0] % 2 == 1
    pack_ref[pl.ds(0, half), :] = jnp.where(odd, other_ref[...], mine_ref[...])
    pack_ref[pl.ds(half, half), :] = jnp.where(odd, mine_ref[...], other_ref[...])
    pairs, blocks = pack_layout(tiles)
    down, across = square_iota(0), square_iota(1)

    def square(tile):
        return pl.ds(tile * LANES, LANES), pl.ds(tile * LANES, LANES)

    for first, at, line in pairs:
        folded = pack_ref[pl.ds(at, LANES), :]
        turned = folded.T
        a_ref[square(first)] = jnp.where(down <= across, folded, turned)
        diagonal = jnp.broadcast_to(pack_ref[pl.ds(line, 1), :], (LANES, LANES))
        value = jnp.where(down > across, folded, turned)
        a_ref[square(first + 1)] = jnp.where(down == across, diagonal, value)
    for row, col, at in blocks:
        a_ref[pl.ds(row * LANES, LANES), pl.ds(col * LANES, LANES)] = pack_ref[pl.ds(at, LANES), :]
    rows_iota = lax.broadcasted_iota(jnp.int32, (size, size), 0)
    cols_iota = lax.broadcasted_iota(jnp.int32, (size, size), 1)
    w_ref[...] = jnp.where(rows_iota == cols_iota, 1.0, 0.0)

    for base in range(0, size, BLOCK):
        tile, offset = divmod(base, LANES)
        a_tiles, w_tiles = range(tile, tiles), range(tile + 1)
        places = [(a_ref, t) for t in a_tiles] + [(w_ref, t) for t in w_tiles]
        panel = [
            [ref[pl.ds(base + g, SUB), pl.ds(t * LANES, LANES)] for g in range(0, BLOCK, SUB)] for ref, t in places
        ]
        panel = [jnp.concatenate(lanes, axis=0) for lanes in eliminate(panel, offset)]
        for (ref, t), value in zip(places, panel):
            ref[pl.ds(base, BLOCK), pl.ds(t * LANES, LANES)] = value
        after = base + BLOCK
        if after == size:
            break
        parts = [wide_split(value) for value in panel]
        left = [jnp.concatenate([a, a, b], axis=0) for a, b in parts[: len(a_tiles)]]
        right = [jnp.concatenate([a, b, a], axis=0) for a, b in parts]
        for row_tile in a_tiles:
            skip = after - row_tile * LANES if after > row_tile * LANES else 0
            if skip == LANES:
                continue
            rows = pl.ds(row_tile * LANES + skip, LANES - skip)
            for (ref, t), value in zip(places, right):
                if ref is a_ref and t < row_tile:
                    continue
                update = tn_dot(left[row_tile - tile], value)
                lanes = pl.ds(t * LANES, LANES)
                ref[rows, lanes] = ref[rows, lanes] - update[skip:, :]

    lower = rows_iota[:LANES, :LANES] >= cols_iota[:LANES, :LANES]
    for row in range(tiles):
        for col in range(tiles):
            into = (pl.ds(row * LANES, LANES), pl.ds(col * LANES, LANES))
            if row < col:
                factor_ref[into] = jnp.zeros((LANES, LANES), jnp.float32)
                continue
            block = a_ref[pl.ds(col * LANES, LANES), pl.ds(row * LANES, LANES)].T
            factor_ref[into] = jnp.where(lower, block, 0.0) if row == col else block
    chunk = 256
    for row in range(tiles):
        depth = (row + 1) * LANES
        rows = pl.ds(row * LANES, LANES)
        high, rest = wide_split(w_ref[rows, pl.ds(0, depth)])
        for start in range(0, out_ref.shape[1], chunk):
            cols = pl.ds(start, chunk)
            right_high, right_rest = high_ref[pl.ds(0, depth), cols], rest_ref[pl.ds(0, depth), cols]
            value = jnp.dot(high, right_high, preferred_element_type=jnp.float32)
            value += jnp.dot(high, right_rest, preferred_element_type=jnp.float32)
            value += jnp.dot(rest, right_high, preferred_element_type=jnp.float32)
            out_ref[rows, cols] = value.astype(jnp.bfloat16)


def call(kernel, outs, scratch, flops, grant, whole=0):
    vmem = pl.BlockSpec(memory_space=pltpu.VMEM)
    smem = pl.BlockSpec(memory_space=pltpu.SMEM)
    hbm = pl.BlockSpec(memory_space=pltpu.HBM)

    def run(scalar, *args):
        size = sum(math.prod(x.shape) * x.dtype.itemsize for x in (*args, *outs))
        args = [pltpu.with_memory_space_constraint(x, pltpu.HBM) for x in args[:whole]] + list(args[whole:])
        return pl.pallas_call(
            kernel,
            out_shape=outs,
            in_specs=[smem] + [hbm] * whole + [vmem] * (len(args) - whole),
            out_specs=[vmem] * len(outs),
            scratch_shapes=scratch,
            compiler_params=pltpu.CompilerParams(vmem_limit_bytes=grant << 20),
            cost_estimate=pl.CostEstimate(flops=flops, bytes_accessed=size, transcendentals=0),
        )(scalar, *args)

    return run


def shape(dtype, *dims):
    return jax.ShapeDtypeStruct(dims, dtype)


def compute(basis_cols, snapshots):
    snaps, row_points = snapshots.shape
    modes = basis_cols.shape[1]
    row_index, column_index = lax.axis_index("rows"), lax.axis_index("cols")
    row_count, columns = lax.axis_size("rows"), lax.axis_size("cols")
    total_points = row_points * row_count
    points = row_points // columns
    half = snaps // 2
    bf16, f32 = jnp.bfloat16, jnp.float32

    row_bits = bits(row_count, columns)
    sum_steps = list(zip(row_bits, row_bits[1:] + row_bits[:1]))
    flat = row_index * columns + column_index
    odd = (flat // jnp.where(column_index % 2 == 0, sum_steps[0][0], sum_steps[0][1])) % 2
    place = jnp.stack([column_index, odd]).astype(jnp.int32)

    slab, part = shape(bf16, points, modes), shape(f32, half, modes)
    semaphores = pltpu.SemaphoreType.DMA((columns,))
    kept, sent, *slabs, own_snaps = call(
        project_kernel,
        (part, part) + (slab,) * columns + (shape(bf16, snaps, points),),
        [pltpu.VMEM((snaps, points), bf16)] * (columns - 1) + [semaphores, semaphores],
        2 * snaps * row_points * modes,
        12,
        2,
    )(place, basis_cols, snapshots)
    arrived_slabs = [swap(slabs[offset], (offset,) * 2) for offset in range(2, columns)]
    own_slab, near_slab = slabs[:2]
    arrived = swap(sent, sum_steps[0])
    near_slab = swap(near_slab, (1, 1))
    kept = kept + arrived
    for step in sum_steps[1:]:
        kept = kept + swap(kept, step)
    low = (kept * (math.sqrt(RANK) / total_points)).astype(bf16)
    other = swap(low, sum_steps[0])
    low = jnp.concatenate([jnp.where(odd == 1, other, low), jnp.where(odd == 1, low, other)], 0)
    lows = {0: low}
    for offset in range(2, columns, 2):
        lows[offset] = swap(low, (offset, offset))
    for offset in range(0, columns, 2):
        lows[offset + 1] = swap(lows[offset], (1, 1))

    begun, coefficients = call(
        recon_kernel, (shape(f32, snaps, points), shape(f32, modes, snaps)), [], 4 * snaps * points * modes, 8
    )(place, lows[0], lows[1], own_slab, near_slab)
    packed = packed_rows(snaps // LANES)
    part = shape(f32, packed // 2, LANES)
    wide = shape(bf16, snaps, points)
    high, rest, keep, send = call(
        functools.partial(residual_kernel, total_points),
        (wide, wide, part, part),
        [pltpu.VMEM((packed, LANES), f32)],
        2 * snaps * points * (modes * (columns - 2) + 3 * snaps),
        16,
    )(place, *[lows[offset] for offset in range(2, columns)], *arrived_slabs, begun, own_snaps)
    keep = keep + swap(send, (1, 1))
    for masks in zip(*exchange_rounds(bits(columns // 2, 2) + row_bits)):
        if masks[0][1] == 0:
            keep = keep + swap(keep, [mask[0] for mask in masks])
            continue
        far = swap(keep, [mask[1] for mask in masks])
        diagonal = swap(keep, [mask[0] ^ mask[1] for mask in masks])
        keep = (keep + swap(keep, [mask[0] for mask in masks])) + (far + diagonal)
    rest_of_gram = swap(keep, (1, 1))
    factor, directions = call(
        factor_kernel,
        (shape(f32, snaps, snaps), wide),
        [pltpu.VMEM((snaps, snaps), f32)] * 2 + [pltpu.VMEM((packed, LANES), f32)],
        6 * snaps * snaps * points,
        16,
    )(place, keep, rest_of_gram, high, rest)
    return (coefficients, factor, directions)


def solution(mesh):
    placed = (P("rows", "cols"), P(None, "rows"))
    return jax.shard_map(
        compute,
        mesh=mesh,
        in_specs=placed,
        out_specs=(P("cols", None), P(), P(None, ("rows", "cols"))),
        check_vma=False,
    )
```

```python
import functools
import math

import jax
import jax.numpy as jnp
from jax import lax
from jax.experimental import pallas as pl
from jax.experimental.pallas import tpu as pltpu
from jax.sharding import PartitionSpec as P


RANK = 1024
LANES = 128
BLOCK = 64
STEP = 16
SUB = 8


def swap(value, masks):
    count = lax.axis_size("rows") * lax.axis_size("cols")
    return lax.ppermute(value, ("rows", "cols"), [(i, i ^ masks[i % 2]) for i in range(count)])


def bits(count, step=1):
    found = []
    while count > 1:
        found.append(step)
        step, count = 2 * step, count // 2
    return found


def exchange_rounds(masks):
    rounds = [(masks[at], masks[at + 1] if at + 1 < len(masks) else 0) for at in range(0, len(masks), 2)]
    paired = [pair for pair in rounds if pair[1]]
    single = [pair for pair in rounds if not pair[1]]
    return paired + single, paired[::-1] + single


def wide_split(value):
    high = value.astype(jnp.bfloat16)
    return high, (value - high.astype(jnp.float32)).astype(jnp.bfloat16)


def nt_dot(left, right):
    return lax.dot_general(left, right, (((1,), (1,)), ((), ())), preferred_element_type=jnp.float32)


def tn_dot(left, right):
    return lax.dot_general(left, right, (((0,), (0,)), ((), ())), preferred_element_type=jnp.float32)


def slab_copies(place_ref, whole_ref, into_refs, sem_ref, first, by_rows):
    copies = []
    for index, into_ref in enumerate(into_refs):
        size = into_ref.shape[0 if by_rows else 1]
        start = pl.multiple_of((place_ref[0] ^ (first + index)) * size, size)
        span = whole_ref.at[pl.ds(start, size), :] if by_rows else whole_ref.at[:, pl.ds(start, size)]
        copies.append(pltpu.make_async_copy(span, into_ref, sem_ref.at[index]))
    return copies


def slab_kernel(place_ref, basis_ref, *refs):
    copies = slab_copies(place_ref, basis_ref, refs[:-1], refs[-1], 2, True)
    for copy in copies:
        copy.start()
    for copy in copies:
        copy.wait()


def project_kernel(place_ref, basis_ref, snaps_ref, *refs):
    count = (len(refs) - 4) // 2
    far_refs = refs[: count - 2]
    keep_ref, send_ref, near_ref, own_ref = refs[count - 2 : count + 2]
    part_refs, basis_sem, snaps_sem = refs[count + 2 : -2], refs[-2], refs[-1]
    basis_copies = slab_copies(place_ref, basis_ref, (own_ref, near_ref), basis_sem, 0, True)
    snaps_copies = slab_copies(place_ref, snaps_ref, part_refs, snaps_sem, 0, False)
    for copy in snaps_copies[2:] + basis_copies + snaps_copies[:2]:
        copy.start()
    total = None
    order = list(range(2, count)) + [0, 1]
    slab_refs = (own_ref, near_ref) + tuple(far_refs)
    for offset in order:
        snaps_copies[offset].wait()
        if offset < 2:
            basis_copies[offset].wait()
        value = jnp.dot(part_refs[offset][...], slab_refs[offset][...], preferred_element_type=jnp.float32)
        total = value if total is None else total + value
    half = total.shape[0] // 2
    odd = place_ref[1] == 1
    first, second = total[:half, :], total[half:, :]
    keep_ref[...] = jnp.where(odd, second, first)
    send_ref[...] = jnp.where(odd, first, second)


def recon_kernel(place_ref, basis_ref, low_ref, near_low_ref, near_ref, recon_ref, coefficients_ref, own_ref, sem_ref):
    (copy,) = slab_copies(place_ref, basis_ref, (own_ref,), sem_ref, 0, True)
    copy.start()
    coefficients_ref[...] = low_ref[...].astype(jnp.float32).T
    copy.wait()
    chunk = 256
    for start in range(0, recon_ref.shape[1], chunk):
        cols = slice(start, start + chunk)
        recon_ref[:, cols] = nt_dot(low_ref[...], own_ref[cols, :]) + nt_dot(near_low_ref[...], near_ref[cols, :])


def packed_rows(tiles):
    return tiles // 2 * (LANES + 2 * SUB) + tiles * (tiles - 1) // 2 * LANES


def pack_layout(tiles):
    at, pairs, blocks = 0, [], []
    for first in range(0, tiles, 2):
        pairs.append((first, at, at + LANES))
        at += LANES + 2 * SUB
    for row in range(tiles):
        for col in range(row + 1, tiles):
            blocks.append((row, col, at))
            at += LANES
    return pairs, blocks


def square_iota(dim):
    return lax.broadcasted_iota(jnp.int32, (LANES, LANES), dim)


def residual_kernel(total_points, place_ref, whole_ref, *refs):
    count = (len(refs) - 8) // 2
    low_refs, basis_refs = refs[:count], refs[count : 2 * count]
    begun_ref, high_ref, rest_ref, keep_ref, send_ref, pack_ref, snaps_ref, sem_ref = refs[2 * count :]
    (copy,) = slab_copies(place_ref, whole_ref, (snaps_ref,), sem_ref, 0, False)
    copy.start()
    snaps, points = snaps_ref.shape
    chunk = 256
    for start in range(0, points, chunk):
        cols = slice(start, start + chunk)
        recon = begun_ref[:, cols]
        for low_ref, basis_ref in zip(low_refs, basis_refs):
            recon += nt_dot(low_ref[...], basis_ref[cols, :])
        if start == 0:
            copy.wait()
        residual = snaps_ref[:, cols].astype(jnp.float32) - recon * (1.0 / math.sqrt(RANK))
        high, rest = wide_split(residual)
        high_ref[:, cols] = high
        rest_ref[:, cols] = rest
    scale = 1.0 / total_points

    def block(row, col):
        rows, cols = pl.ds(row * LANES, LANES), pl.ds(col * LANES, LANES)
        value = nt_dot(high_ref[rows, :], high_ref[cols, :])
        value += nt_dot(high_ref[rows, :], rest_ref[cols, :]) + nt_dot(rest_ref[rows, :], high_ref[cols, :])
        return value * scale

    pairs, blocks = pack_layout(snaps // LANES)
    down, across = square_iota(0), square_iota(1)
    for first, at, line in pairs:
        upper, lower = block(first, first), block(first + 1, first + 1)
        pack_ref[pl.ds(at, LANES), :] = jnp.where(down <= across, upper, lower)
        diagonal = jnp.sum(jnp.where(down == across, lower, 0.0), axis=0, keepdims=True)
        pack_ref[pl.ds(line, 2 * SUB), :] = jnp.broadcast_to(diagonal, (2 * SUB, LANES))
    for row, col, at in blocks:
        pack_ref[pl.ds(at, LANES), :] = block(row, col)
    half = pack_ref.shape[0] // 2
    odd = place_ref[0] % 2 == 1
    first, second = pack_ref[pl.ds(0, half), :], pack_ref[pl.ds(half, half), :]
    keep_ref[...] = jnp.where(odd, second, first)
    send_ref[...] = jnp.where(odd, first, second)


def row_of(tile, index):
    return jnp.broadcast_to(tile[index : index + 1, :], tile.shape)


def eliminate(panel, offset):
    groups = BLOCK // SUB
    sub_iota = lax.broadcasted_iota(jnp.int32, (SUB, LANES), 0)
    scales = [jnp.zeros((SUB, LANES), jnp.float32) for _ in range(groups)]
    for begin in range(0, BLOCK, STEP):
        columns = [
            [
                jnp.broadcast_to(panel[0][g][:, offset + j : offset + j + 1], (SUB, LANES))
                if g >= begin // SUB
                else None
                for g in range(groups)
            ]
            for j in range(begin, begin + STEP)
        ]
        for p in range(begin, begin + STEP):
            home, line = divmod(p, SUB)
            column = columns[p - begin]
            pivot = row_of(column[home], line)
            inverse = 1.0 / pivot
            scales[home] = jnp.where(sub_iota == line, lax.rsqrt(pivot), scales[home])
            factors = {}
            for g in range(home, groups):
                value = column[g] * inverse
                if g == home:
                    if line == SUB - 1:
                        continue
                    value = jnp.where(sub_iota > line, value, 0.0)
                factors[g] = value
            for lanes in columns[p - begin + 1 :] + panel:
                lead = row_of(lanes[home], line)
                for g, value in factors.items():
                    lanes[g] = lanes[g] - value * lead
    return [[tile * scale for tile, scale in zip(lanes, scales)] for lanes in panel]


def factor_kernel(place_ref, mine_ref, other_ref, high_ref, rest_ref, factor_ref, out_ref, a_ref, w_ref, pack_ref):
    size = factor_ref.shape[0]
    tiles = size // LANES
    half = mine_ref.shape[0]
    odd = place_ref[0] % 2 == 1
    pack_ref[pl.ds(0, half), :] = jnp.where(odd, other_ref[...], mine_ref[...])
    pack_ref[pl.ds(half, half), :] = jnp.where(odd, mine_ref[...], other_ref[...])
    pairs, blocks = pack_layout(tiles)
    down, across = square_iota(0), square_iota(1)

    def square(tile):
        return pl.ds(tile * LANES, LANES), pl.ds(tile * LANES, LANES)

    for first, at, line in pairs:
        folded = pack_ref[pl.ds(at, LANES), :]
        turned = folded.T
        a_ref[square(first)] = jnp.where(down <= across, folded, turned)
        diagonal = jnp.broadcast_to(pack_ref[pl.ds(line, 1), :], (LANES, LANES))
        value = jnp.where(down > across, folded, turned)
        a_ref[square(first + 1)] = jnp.where(down == across, diagonal, value)
    for row, col, at in blocks:
        a_ref[pl.ds(row * LANES, LANES), pl.ds(col * LANES, LANES)] = pack_ref[pl.ds(at, LANES), :]
    rows_iota = lax.broadcasted_iota(jnp.int32, (size, size), 0)
    cols_iota = lax.broadcasted_iota(jnp.int32, (size, size), 1)
    w_ref[...] = jnp.where(rows_iota == cols_iota, 1.0, 0.0)

    for base in range(0, size, BLOCK):
        tile, offset = divmod(base, LANES)
        a_tiles, w_tiles = range(tile, tiles), range(tile + 1)
        places = [(a_ref, t) for t in a_tiles] + [(w_ref, t) for t in w_tiles]
        panel = [
            [ref[pl.ds(base + g, SUB), pl.ds(t * LANES, LANES)] for g in range(0, BLOCK, SUB)] for ref, t in places
        ]
        panel = [jnp.concatenate(lanes, axis=0) for lanes in eliminate(panel, offset)]
        for (ref, t), value in zip(places, panel):
            ref[pl.ds(base, BLOCK), pl.ds(t * LANES, LANES)] = value
        after = base + BLOCK
        if after == size:
            break
        parts = [wide_split(value) for value in panel]
        left = [jnp.concatenate([a, a, b], axis=0) for a, b in parts[: len(a_tiles)]]
        right = [jnp.concatenate([a, b, a], axis=0) for a, b in parts]
        for row_tile in a_tiles:
            skip = after - row_tile * LANES if after > row_tile * LANES else 0
            if skip == LANES:
                continue
            rows = pl.ds(row_tile * LANES + skip, LANES - skip)
            for (ref, t), value in zip(places, right):
                if ref is a_ref and t < row_tile:
                    continue
                update = tn_dot(left[row_tile - tile], value)
                lanes = pl.ds(t * LANES, LANES)
                ref[rows, lanes] = ref[rows, lanes] - update[skip:, :]

    lower = rows_iota[:LANES, :LANES] >= cols_iota[:LANES, :LANES]
    for row in range(tiles):
        for col in range(tiles):
            into = (pl.ds(row * LANES, LANES), pl.ds(col * LANES, LANES))
            if row < col:
                factor_ref[into] = jnp.zeros((LANES, LANES), jnp.float32)
                continue
            block = a_ref[pl.ds(col * LANES, LANES), pl.ds(row * LANES, LANES)].T
            factor_ref[into] = jnp.where(lower, block, 0.0) if row == col else block
    chunk = 256
    for row in range(tiles):
        depth = (row + 1) * LANES
        rows = pl.ds(row * LANES, LANES)
        high, rest = wide_split(w_ref[rows, pl.ds(0, depth)])
        for start in range(0, out_ref.shape[1], chunk):
            cols = pl.ds(start, chunk)
            right_high, right_rest = high_ref[pl.ds(0, depth), cols], rest_ref[pl.ds(0, depth), cols]
            value = jnp.dot(high, right_high, preferred_element_type=jnp.float32)
            value += jnp.dot(high, right_rest, preferred_element_type=jnp.float32)
            value += jnp.dot(rest, right_high, preferred_element_type=jnp.float32)
            out_ref[rows, cols] = value.astype(jnp.bfloat16)


def call(kernel, outs, scratch, flops, grant, whole=0):
    vmem = pl.BlockSpec(memory_space=pltpu.VMEM)
    smem = pl.BlockSpec(memory_space=pltpu.SMEM)
    hbm = pl.BlockSpec(memory_space=pltpu.HBM)

    def run(scalar, *args):
        size = sum(math.prod(x.shape) * x.dtype.itemsize for x in (*args, *outs))
        args = [pltpu.with_memory_space_constraint(x, pltpu.HBM) for x in args[:whole]] + list(args[whole:])
        return pl.pallas_call(
            kernel,
            out_shape=outs,
            in_specs=[smem] + [hbm] * whole + [vmem] * (len(args) - whole),
            out_specs=[vmem] * len(outs),
            scratch_shapes=scratch,
            compiler_params=pltpu.CompilerParams(vmem_limit_bytes=grant << 20),
            cost_estimate=pl.CostEstimate(flops=flops, bytes_accessed=size, transcendentals=0),
        )(scalar, *args)

    return run


def shape(dtype, *dims):
    return jax.ShapeDtypeStruct(dims, dtype)


def compute(basis_cols, snapshots):
    snaps, row_points = snapshots.shape
    modes = basis_cols.shape[1]
    row_index, column_index = lax.axis_index("rows"), lax.axis_index("cols")
    row_count, columns = lax.axis_size("rows"), lax.axis_size("cols")
    total_points = row_points * row_count
    points = row_points // columns
    half = snaps // 2
    bf16, f32 = jnp.bfloat16, jnp.float32

    row_bits = bits(row_count, columns)
    sum_steps = list(zip(row_bits, row_bits[1:] + row_bits[:1]))
    flat = row_index * columns + column_index
    odd = (flat // jnp.where(column_index % 2 == 0, sum_steps[0][0], sum_steps[0][1])) % 2
    place = jnp.stack([column_index, odd]).astype(jnp.int32)

    slab, part = shape(bf16, points, modes), shape(f32, half, modes)
    slab_scratch, span_scratch = pltpu.VMEM((points, modes), bf16), pltpu.VMEM((snaps, points), bf16)
    semaphores = pltpu.SemaphoreType.DMA((columns,))
    far_slabs = call(slab_kernel, (slab,) * (columns - 2), [semaphores], 0, 4, 1)(place, basis_cols)
    arrived_slabs = [swap(far_slabs[at], (2 + at,) * 2) for at in range(columns - 2)]
    kept, sent, near_slab = call(
        project_kernel,
        (part, part, slab),
        [slab_scratch] + [span_scratch] * columns + [semaphores, semaphores],
        2 * snaps * row_points * modes,
        12,
        2,
    )(place, basis_cols, snapshots, *far_slabs)
    arrived = swap(sent, sum_steps[0])
    near_slab = swap(near_slab, (1, 1))
    kept = kept + arrived
    for step in sum_steps[1:]:
        kept = kept + swap(kept, step)
    low = (kept * (math.sqrt(RANK) / total_points)).astype(bf16)
    other = swap(low, sum_steps[0])
    low = jnp.concatenate([jnp.where(odd == 1, other, low), jnp.where(odd == 1, low, other)], 0)
    lows = {0: low}
    for offset in range(2, columns, 2):
        lows[offset] = swap(low, (offset, offset))
    for offset in range(0, columns, 2):
        lows[offset + 1] = swap(lows[offset], (1, 1))

    begun, coefficients = call(
        recon_kernel,
        (shape(f32, snaps, points), shape(f32, modes, snaps)),
        [slab_scratch, semaphores],
        4 * snaps * points * modes,
        8,
        1,
    )(place, basis_cols, lows[0], lows[1], near_slab)
    packed = packed_rows(snaps // LANES)
    part = shape(f32, packed // 2, LANES)
    wide = shape(bf16, snaps, points)
    high, rest, keep, send = call(
        functools.partial(residual_kernel, total_points),
        (wide, wide, part, part),
        [pltpu.VMEM((packed, LANES), f32), span_scratch, semaphores],
        2 * snaps * points * (modes * (columns - 2) + 3 * snaps),
        16,
        1,
    )(place, snapshots, *[lows[offset] for offset in range(2, columns)], *arrived_slabs, begun)
    keep = keep + swap(send, (1, 1))
    for masks in zip(*exchange_rounds(bits(columns // 2, 2) + row_bits)):
        if masks[0][1] == 0:
            keep = keep + swap(keep, [mask[0] for mask in masks])
            continue
        far = swap(keep, [mask[1] for mask in masks])
        diagonal = swap(keep, [mask[0] ^ mask[1] for mask in masks])
        keep = (keep + swap(keep, [mask[0] for mask in masks])) + (far + diagonal)
    rest_of_gram = swap(keep, (1, 1))
    factor, directions = call(
        factor_kernel,
        (shape(f32, snaps, snaps), wide),
        [pltpu.VMEM((snaps, snaps), f32)] * 2 + [pltpu.VMEM((packed, LANES), f32)],
        6 * snaps * snaps * points,
        16,
    )(place, keep, rest_of_gram, high, rest)
    return (coefficients, factor, directions)


def solution(mesh):
    placed = (P("rows", "cols"), P(None, "rows"))
    return jax.shard_map(
        compute,
        mesh=mesh,
        in_specs=placed,
        out_specs=(P("cols", None), P(), P(None, ("rows", "cols"))),
        check_vma=False,
    )
```

```python
import functools
import math

import jax
import jax.numpy as jnp
from jax import lax
from jax.experimental import pallas as pl
from jax.experimental.pallas import tpu as pltpu
from jax.sharding import PartitionSpec as P


RANK = 1024
LANES = 128
BLOCK = 64
STEP = 16
SUB = 8


def swap(value, masks):
    count = lax.axis_size("rows") * lax.axis_size("cols")
    return lax.ppermute(value, ("rows", "cols"), [(i, i ^ masks[i % 2]) for i in range(count)])


def bits(count, step=1):
    found = []
    while count > 1:
        found.append(step)
        step, count = 2 * step, count // 2
    return found


def exchange_rounds(masks):
    rounds = [(masks[at], masks[at + 1] if at + 1 < len(masks) else 0) for at in range(0, len(masks), 2)]
    paired = [pair for pair in rounds if pair[1]]
    single = [pair for pair in rounds if not pair[1]]
    return paired + single, paired[::-1] + single


def wide_split(value):
    high = value.astype(jnp.bfloat16)
    return high, (value - high.astype(jnp.float32)).astype(jnp.bfloat16)


def nt_dot(left, right):
    return lax.dot_general(left, right, (((1,), (1,)), ((), ())), preferred_element_type=jnp.float32)


def tn_dot(left, right):
    return lax.dot_general(left, right, (((0,), (0,)), ((), ())), preferred_element_type=jnp.float32)


def slab_copies(place_ref, whole_ref, into_refs, sem_ref, first, by_rows):
    copies = []
    for index, into_ref in enumerate(into_refs):
        size = into_ref.shape[0 if by_rows else 1]
        start = pl.multiple_of((place_ref[0] ^ (first + index)) * size, size)
        span = whole_ref.at[pl.ds(start, size), :] if by_rows else whole_ref.at[:, pl.ds(start, size)]
        copies.append(pltpu.make_async_copy(span, into_ref, sem_ref.at[index]))
    return copies


def project_kernel(place_ref, basis_ref, snaps_ref, *refs):
    count = (len(refs) - 7) // 2
    piece_refs, slab_refs = refs[:4], (refs[3 + count],) + refs[4 : 3 + count]
    part_refs, total_ref, basis_sem, snaps_sem = refs[4 + count : 4 + 2 * count], refs[-3], refs[-2], refs[-1]
    basis_copies = slab_copies(place_ref, basis_ref, slab_refs, basis_sem, 0, True)
    snaps_copies = slab_copies(place_ref, snaps_ref, part_refs, snaps_sem, 0, False)
    for pair in zip(basis_copies, snaps_copies):
        for copy in pair:
            copy.start()
    total = None
    for offset in range(count):
        basis_copies[offset].wait()
        snaps_copies[offset].wait()
        value = jnp.dot(part_refs[offset][...], slab_refs[offset][...], preferred_element_type=jnp.float32)
        total = value if total is None else total + value
    total_ref[...] = total
    rows = piece_refs[0].shape[0]
    for offset, piece_ref in enumerate(piece_refs):
        start = pl.multiple_of((place_ref[1] ^ offset) * rows, rows)
        piece_ref[...] = total_ref[pl.ds(start, rows), :]


def recon_kernel(place_ref, basis_ref, snaps_ref, low_ref, near_low_ref, near_ref, base_ref, coefficients_ref, *scratch):
    own_ref, span_ref, basis_sem, snaps_sem = scratch
    (basis_copy,) = slab_copies(place_ref, basis_ref, (own_ref,), basis_sem, 0, True)
    (snaps_copy,) = slab_copies(place_ref, snaps_ref, (span_ref,), snaps_sem, 0, False)
    basis_copy.start()
    snaps_copy.start()
    coefficients_ref[...] = low_ref[...].astype(jnp.float32).T
    basis_copy.wait()
    snaps_copy.wait()
    chunk = 256
    for start in range(0, base_ref.shape[1], chunk):
        cols = slice(start, start + chunk)
        recon = nt_dot(low_ref[...], own_ref[cols, :]) + nt_dot(near_low_ref[...], near_ref[cols, :])
        base_ref[:, cols] = span_ref[:, cols].astype(jnp.float32) - recon * (1.0 / math.sqrt(RANK))


def packed_rows(tiles):
    return tiles // 2 * (LANES + 2 * SUB) + tiles * (tiles - 1) // 2 * LANES


def pack_layout(tiles):
    at, pairs, blocks = 0, [], []
    for first in range(0, tiles, 2):
        pairs.append((first, at, at + LANES))
        at += LANES + 2 * SUB
    for row in range(tiles):
        for col in range(row + 1, tiles):
            blocks.append((row, col, at))
            at += LANES
    return pairs, blocks


def square_iota(dim):
    return lax.broadcasted_iota(jnp.int32, (LANES, LANES), dim)


def residual_kernel(total_points, place_ref, *refs):
    count = (len(refs) - 6) // 2
    low_refs, basis_refs = refs[:count], refs[count : 2 * count]
    base_ref, high_ref, rest_ref, keep_ref, send_ref, pack_ref = refs[2 * count :]
    snaps, points = base_ref.shape
    chunk = 256
    for start in range(0, points, chunk):
        cols = slice(start, start + chunk)
        recon = nt_dot(low_refs[0][...], basis_refs[0][cols, :])
        for low_ref, basis_ref in zip(low_refs[1:], basis_refs[1:]):
            recon += nt_dot(low_ref[...], basis_ref[cols, :])
        high, rest = wide_split(base_ref[:, cols] - recon * (1.0 / math.sqrt(RANK)))
        high_ref[:, cols] = high
        rest_ref[:, cols] = rest
    scale = 1.0 / total_points

    def block(row, col):
        rows, cols = pl.ds(row * LANES, LANES), pl.ds(col * LANES, LANES)
        value = nt_dot(high_ref[rows, :], high_ref[cols, :])
        value += nt_dot(high_ref[rows, :], rest_ref[cols, :]) + nt_dot(rest_ref[rows, :], high_ref[cols, :])
        return value * scale

    pairs, blocks = pack_layout(snaps // LANES)
    down, across = square_iota(0), square_iota(1)
    for first, at, line in pairs:
        upper, lower = block(first, first), block(first + 1, first + 1)
        pack_ref[pl.ds(at, LANES), :] = jnp.where(down <= across, upper, lower)
        diagonal = jnp.sum(jnp.where(down == across, lower, 0.0), axis=0, keepdims=True)
        pack_ref[pl.ds(line, 2 * SUB), :] = jnp.broadcast_to(diagonal, (2 * SUB, LANES))
    for row, col, at in blocks:
        pack_ref[pl.ds(at, LANES), :] = block(row, col)
    half = pack_ref.shape[0] // 2
    odd = place_ref[0] % 2 == 1
    first, second = pack_ref[pl.ds(0, half), :], pack_ref[pl.ds(half, half), :]
    keep_ref[...] = jnp.where(odd, second, first)
    send_ref[...] = jnp.where(odd, first, second)


def row_of(tile, index):
    return jnp.broadcast_to(tile[index : index + 1, :], tile.shape)


def eliminate(panel, offset):
    groups = BLOCK // SUB
    sub_iota = lax.broadcasted_iota(jnp.int32, (SUB, LANES), 0)
    scales = [jnp.zeros((SUB, LANES), jnp.float32) for _ in range(groups)]
    for begin in range(0, BLOCK, STEP):
        columns = [
            [
                jnp.broadcast_to(panel[0][g][:, offset + j : offset + j + 1], (SUB, LANES))
                if g >= begin // SUB
                else None
                for g in range(groups)
            ]
            for j in range(begin, begin + STEP)
        ]
        for p in range(begin, begin + STEP):
            home, line = divmod(p, SUB)
            column = columns[p - begin]
            pivot = row_of(column[home], line)
            inverse = 1.0 / pivot
            scales[home] = jnp.where(sub_iota == line, lax.rsqrt(pivot), scales[home])
            factors = {}
            for g in range(home, groups):
                value = column[g] * inverse
                if g == home:
                    if line == SUB - 1:
                        continue
                    value = jnp.where(sub_iota > line, value, 0.0)
                factors[g] = value
            for lanes in columns[p - begin + 1 :] + panel:
                lead = row_of(lanes[home], line)
                for g, value in factors.items():
                    lanes[g] = lanes[g] - value * lead
    return [[tile * scale for tile, scale in zip(lanes, scales)] for lanes in panel]


def factor_kernel(place_ref, mine_ref, other_ref, high_ref, rest_ref, factor_ref, out_ref, a_ref, w_ref, pack_ref):
    size = factor_ref.shape[0]
    tiles = size // LANES
    half = mine_ref.shape[0]
    odd = place_ref[0] % 2 == 1
    pack_ref[pl.ds(0, half), :] = jnp.where(odd, other_ref[...], mine_ref[...])
    pack_ref[pl.ds(half, half), :] = jnp.where(odd, mine_ref[...], other_ref[...])
    pairs, blocks = pack_layout(tiles)
    down, across = square_iota(0), square_iota(1)

    def square(tile):
        return pl.ds(tile * LANES, LANES), pl.ds(tile * LANES, LANES)

    for first, at, line in pairs:
        folded = pack_ref[pl.ds(at, LANES), :]
        turned = folded.T
        a_ref[square(first)] = jnp.where(down <= across, folded, turned)
        diagonal = jnp.broadcast_to(pack_ref[pl.ds(line, 1), :], (LANES, LANES))
        value = jnp.where(down > across, folded, turned)
        a_ref[square(first + 1)] = jnp.where(down == across, diagonal, value)
    for row, col, at in blocks:
        a_ref[pl.ds(row * LANES, LANES), pl.ds(col * LANES, LANES)] = pack_ref[pl.ds(at, LANES), :]
    rows_iota = lax.broadcasted_iota(jnp.int32, (size, size), 0)
    cols_iota = lax.broadcasted_iota(jnp.int32, (size, size), 1)
    w_ref[...] = jnp.where(rows_iota == cols_iota, 1.0, 0.0)

    for base in range(0, size, BLOCK):
        tile, offset = divmod(base, LANES)
        a_tiles, w_tiles = range(tile, tiles), range(tile + 1)
        places = [(a_ref, t) for t in a_tiles] + [(w_ref, t) for t in w_tiles]
        panel = [
            [ref[pl.ds(base + g, SUB), pl.ds(t * LANES, LANES)] for g in range(0, BLOCK, SUB)] for ref, t in places
        ]
        panel = [jnp.concatenate(lanes, axis=0) for lanes in eliminate(panel, offset)]
        for (ref, t), value in zip(places, panel):
            ref[pl.ds(base, BLOCK), pl.ds(t * LANES, LANES)] = value
        after = base + BLOCK
        if after == size:
            break
        parts = [wide_split(value) for value in panel]
        left = [jnp.concatenate([a, a, b], axis=0) for a, b in parts[: len(a_tiles)]]
        right = [jnp.concatenate([a, b, a], axis=0) for a, b in parts]
        for row_tile in a_tiles:
            skip = after - row_tile * LANES if after > row_tile * LANES else 0
            if skip == LANES:
                continue
            rows = pl.ds(row_tile * LANES + skip, LANES - skip)
            for (ref, t), value in zip(places, right):
                if ref is a_ref and t < row_tile:
                    continue
                update = tn_dot(left[row_tile - tile], value)
                lanes = pl.ds(t * LANES, LANES)
                ref[rows, lanes] = ref[rows, lanes] - update[skip:, :]

    lower = rows_iota[:LANES, :LANES] >= cols_iota[:LANES, :LANES]
    for row in range(tiles):
        for col in range(tiles):
            into = (pl.ds(row * LANES, LANES), pl.ds(col * LANES, LANES))
            if row < col:
                factor_ref[into] = jnp.zeros((LANES, LANES), jnp.float32)
                continue
            block = a_ref[pl.ds(col * LANES, LANES), pl.ds(row * LANES, LANES)].T
            factor_ref[into] = jnp.where(lower, block, 0.0) if row == col else block
    chunk = 256
    for row in range(tiles):
        depth = (row + 1) * LANES
        rows = pl.ds(row * LANES, LANES)
        high, rest = wide_split(w_ref[rows, pl.ds(0, depth)])
        for start in range(0, out_ref.shape[1], chunk):
            cols = pl.ds(start, chunk)
            right_high, right_rest = high_ref[pl.ds(0, depth), cols], rest_ref[pl.ds(0, depth), cols]
            value = jnp.dot(high, right_high, preferred_element_type=jnp.float32)
            value += jnp.dot(high, right_rest, preferred_element_type=jnp.float32)
            value += jnp.dot(rest, right_high, preferred_element_type=jnp.float32)
            out_ref[rows, cols] = value.astype(jnp.bfloat16)


def call(kernel, outs, scratch, flops, grant, whole=0):
    vmem = pl.BlockSpec(memory_space=pltpu.VMEM)
    smem = pl.BlockSpec(memory_space=pltpu.SMEM)
    hbm = pl.BlockSpec(memory_space=pltpu.HBM)

    def run(scalar, *args):
        size = sum(math.prod(x.shape) * x.dtype.itemsize for x in (*args, *outs))
        args = [pltpu.with_memory_space_constraint(x, pltpu.HBM) for x in args[:whole]] + list(args[whole:])
        return pl.pallas_call(
            kernel,
            out_shape=outs,
            in_specs=[smem] + [hbm] * whole + [vmem] * (len(args) - whole),
            out_specs=[vmem] * len(outs),
            scratch_shapes=scratch,
            compiler_params=pltpu.CompilerParams(vmem_limit_bytes=grant << 20),
            cost_estimate=pl.CostEstimate(flops=flops, bytes_accessed=size, transcendentals=0),
        )(scalar, *args)

    return run


def shape(dtype, *dims):
    return jax.ShapeDtypeStruct(dims, dtype)


def compute(basis_cols, snapshots):
    snaps, row_points = snapshots.shape
    modes = basis_cols.shape[1]
    row_index, column_index = lax.axis_index("rows"), lax.axis_index("cols")
    row_count, columns = lax.axis_size("rows"), lax.axis_size("cols")
    total_points = row_points * row_count
    points = row_points // columns
    quarter = snaps // 4
    bf16, f32 = jnp.bfloat16, jnp.float32

    row_bits = bits(row_count, columns)
    orders = list(zip(row_bits, row_bits[1:] + row_bits[:1]))
    first, second = orders[0], orders[1]
    both = tuple(a ^ b for a, b in zip(first, second))
    flat = row_index * columns + column_index
    even = column_index % 2 == 0
    low_bit, high_bit = ((flat // jnp.where(even, *masks)) % 2 for masks in (first, second))
    quad = (low_bit + 2 * high_bit).astype(jnp.int32)
    place = jnp.stack([column_index.astype(jnp.int32), quad])

    slab, piece = shape(bf16, points, modes), shape(f32, quarter, modes)
    slab_scratch, span_scratch = pltpu.VMEM((points, modes), bf16), pltpu.VMEM((snaps, points), bf16)
    semaphores = pltpu.SemaphoreType.DMA((columns,))
    kept, one, two, three, *slabs = call(
        project_kernel,
        (piece,) * 4 + (slab,) * (columns - 1),
        [slab_scratch] + [span_scratch] * columns + [pltpu.VMEM((snaps, modes), f32), semaphores, semaphores],
        2 * snaps * row_points * modes,
        12,
        2,
    )(place, basis_cols, snapshots)
    arrived_slabs = [swap(slabs[offset - 1], (offset,) * 2) for offset in range(2, columns)]
    one, two, three = swap(one, first), swap(two, second), swap(three, both)
    near_slab = swap(slabs[0], (1, 1))
    kept = (kept + one) + (two + three)
    for step in orders[2:]:
        kept = kept + swap(kept, step)
    low = (kept * (math.sqrt(RANK) / total_points)).astype(bf16)
    found = (low, swap(low, first), swap(low, second), swap(low, both))
    low = jnp.concatenate([lax.select_n(quad ^ at, *found) for at in range(4)], 0)
    lows = {0: low}
    for offset in range(2, columns, 2):
        lows[offset] = swap(low, (offset, offset))
    for offset in range(0, columns, 2):
        lows[offset + 1] = swap(lows[offset], (1, 1))

    begun, coefficients = call(
        recon_kernel,
        (shape(f32, snaps, points), shape(f32, modes, snaps)),
        [slab_scratch, span_scratch, semaphores, semaphores],
        4 * snaps * points * modes,
        8,
        2,
    )(place, basis_cols, snapshots, lows[0], lows[1], near_slab)
    packed = packed_rows(snaps // LANES)
    part = shape(f32, packed // 2, LANES)
    wide = shape(bf16, snaps, points)
    high, rest, keep, send = call(
        functools.partial(residual_kernel, total_points),
        (wide, wide, part, part),
        [pltpu.VMEM((packed, LANES), f32)],
        2 * snaps * points * (modes * (columns - 2) + 3 * snaps),
        16,
    )(place, *[lows[offset] for offset in range(2, columns)], *arrived_slabs, begun)
    keep = keep + swap(send, (1, 1))
    for masks in zip(*exchange_rounds(bits(columns // 2, 2) + row_bits)):
        if masks[0][1] == 0:
            keep = keep + swap(keep, [mask[0] for mask in masks])
            continue
        far = swap(keep, [mask[1] for mask in masks])
        diagonal = swap(keep, [mask[0] ^ mask[1] for mask in masks])
        keep = (keep + swap(keep, [mask[0] for mask in masks])) + (far + diagonal)
    rest_of_gram = swap(keep, (1, 1))
    factor, directions = call(
        factor_kernel,
        (shape(f32, snaps, snaps), wide),
        [pltpu.VMEM((snaps, snaps), f32)] * 2 + [pltpu.VMEM((packed, LANES), f32)],
        6 * snaps * snaps * points,
        16,
    )(place, keep, rest_of_gram, high, rest)
    return (coefficients, factor, directions)


def solution(mesh):
    placed = (P("rows", "cols"), P(None, "rows"))
    return jax.shard_map(
        compute,
        mesh=mesh,
        in_specs=placed,
        out_specs=(P("cols", None), P(), P(None, ("rows", "cols"))),
        check_vma=False,
    )
```

```python
import functools
import math

import jax
import jax.numpy as jnp
from jax import lax
from jax.experimental import pallas as pl
from jax.experimental.pallas import tpu as pltpu
from jax.sharding import PartitionSpec as P


RANK = 1024
LANES = 128
BLOCK = 32
STEP = 16
SUB = 8


def swap(value, masks):
    count = lax.axis_size("rows") * lax.axis_size("cols")
    return lax.ppermute(value, ("rows", "cols"), [(i, i ^ masks[i % 2]) for i in range(count)])


def bits(count, step=1):
    found = []
    while count > 1:
        found.append(step)
        step, count = 2 * step, count // 2
    return found


def exchange_rounds(masks):
    rounds = [(masks[at], masks[at + 1] if at + 1 < len(masks) else 0) for at in range(0, len(masks), 2)]
    paired = [pair for pair in rounds if pair[1]]
    single = [pair for pair in rounds if not pair[1]]
    return paired + single, paired[::-1] + single


def wide_split(value):
    high = value.astype(jnp.bfloat16)
    return high, (value - high.astype(jnp.float32)).astype(jnp.bfloat16)


def nt_dot(left, right):
    return lax.dot_general(left, right, (((1,), (1,)), ((), ())), preferred_element_type=jnp.float32)


def tn_dot(left, right):
    return lax.dot_general(left, right, (((0,), (0,)), ((), ())), preferred_element_type=jnp.float32)


def slab_copies(whole_ref, into_refs, sem_ref, first, by_rows):
    copies = []
    for index, into_ref in enumerate(into_refs):
        size = into_ref.shape[0 if by_rows else 1]
        start = pl.multiple_of((lax.axis_index("cols") ^ (first + index)) * size, size)
        span = whole_ref.at[pl.ds(start, size), :] if by_rows else whole_ref.at[:, pl.ds(start, size)]
        copies.append(pltpu.make_async_copy(span, into_ref, sem_ref.at[index]))
    return copies


def quad_index(first, second):
    column = lax.axis_index("cols")
    flat = lax.axis_index("rows") * lax.axis_size("cols") + column
    low, high = (flat // jnp.where(column % 2 == 0, *masks) % 2 for masks in (first, second))
    return (low + 2 * high).astype(jnp.int32)


def project_kernel(first, second, basis_ref, snaps_ref, *refs):
    count = (len(refs) - 7) // 2
    piece_refs, slab_refs = refs[:4], (refs[3 + count],) + refs[4 : 3 + count]
    part_refs, total_ref, basis_sem, snaps_sem = refs[4 + count : 4 + 2 * count], refs[-3], refs[-2], refs[-1]
    basis_copies = slab_copies(basis_ref, slab_refs, basis_sem, 0, True)
    snaps_copies = slab_copies(snaps_ref, part_refs, snaps_sem, 0, False)
    for pair in zip(basis_copies, snaps_copies):
        for copy in pair:
            copy.start()
    total = None
    for offset in range(count):
        basis_copies[offset].wait()
        snaps_copies[offset].wait()
        value = jnp.dot(part_refs[offset][...], slab_refs[offset][...], preferred_element_type=jnp.float32)
        total = value if total is None else total + value
    total_ref[...] = total
    rows = piece_refs[0].shape[0]
    quad = quad_index(first, second)
    for offset, piece_ref in enumerate(piece_refs):
        start = pl.multiple_of((quad ^ offset) * rows, rows)
        piece_ref[...] = total_ref[pl.ds(start, rows), :]


def recon_kernel(basis_ref, snaps_ref, low_ref, near_low_ref, near_ref, base_ref, coefficients_ref, *scratch):
    own_ref, span_ref, basis_sem, snaps_sem = scratch
    (basis_copy,) = slab_copies(basis_ref, (own_ref,), basis_sem, 0, True)
    (snaps_copy,) = slab_copies(snaps_ref, (span_ref,), snaps_sem, 0, False)
    basis_copy.start()
    snaps_copy.start()
    coefficients_ref[...] = low_ref[...].astype(jnp.float32).T
    basis_copy.wait()
    snaps_copy.wait()
    chunk = 256
    for start in range(0, base_ref.shape[1], chunk):
        cols = slice(start, start + chunk)
        recon = nt_dot(low_ref[...], own_ref[cols, :]) + nt_dot(near_low_ref[...], near_ref[cols, :])
        base_ref[:, cols] = span_ref[:, cols].astype(jnp.float32) - recon * (1.0 / math.sqrt(RANK))


def packed_rows(tiles):
    return tiles // 2 * (LANES + 2 * SUB) + tiles * (tiles - 1) // 2 * LANES


def pack_layout(tiles):
    at, pairs, blocks = 0, [], []
    for first in range(0, tiles, 2):
        pairs.append((first, at, at + LANES))
        at += LANES + 2 * SUB
    for row in range(tiles):
        for col in range(row + 1, tiles):
            blocks.append((row, col, at))
            at += LANES
    return pairs, blocks


def square_iota(dim):
    return lax.broadcasted_iota(jnp.int32, (LANES, LANES), dim)


def residual_kernel(total_points, *refs):
    count = (len(refs) - 6) // 2
    low_refs, basis_refs = refs[:count], refs[count : 2 * count]
    base_ref, high_ref, rest_ref, keep_ref, send_ref, pack_ref = refs[2 * count :]
    snaps, points = base_ref.shape
    chunk = 256
    for start in range(0, points, chunk):
        cols = slice(start, start + chunk)
        recon = nt_dot(low_refs[0][...], basis_refs[0][cols, :])
        for low_ref, basis_ref in zip(low_refs[1:], basis_refs[1:]):
            recon += nt_dot(low_ref[...], basis_ref[cols, :])
        high, rest = wide_split(base_ref[:, cols] - recon * (1.0 / math.sqrt(RANK)))
        high_ref[:, cols] = high
        rest_ref[:, cols] = rest
    scale = 1.0 / total_points

    high, rest = high_ref[...], rest_ref[...]
    gram = (nt_dot(high, high) + (nt_dot(high, rest) + nt_dot(rest, high))) * scale

    def block(row, col):
        return gram[row * LANES : (row + 1) * LANES, col * LANES : (col + 1) * LANES]

    pairs, blocks = pack_layout(snaps // LANES)
    down, across = square_iota(0), square_iota(1)
    for first, at, line in pairs:
        upper, lower = block(first, first), block(first + 1, first + 1)
        pack_ref[pl.ds(at, LANES), :] = jnp.where(down <= across, upper, lower)
        diagonal = jnp.sum(jnp.where(down == across, lower, 0.0), axis=0, keepdims=True)
        pack_ref[pl.ds(line, 2 * SUB), :] = jnp.broadcast_to(diagonal, (2 * SUB, LANES))
    for row, col, at in blocks:
        pack_ref[pl.ds(at, LANES), :] = block(row, col)
    half = pack_ref.shape[0] // 2
    odd = lax.axis_index("cols") % 2 == 1
    first, second = pack_ref[pl.ds(0, half), :], pack_ref[pl.ds(half, half), :]
    keep_ref[...] = jnp.where(odd, second, first)
    send_ref[...] = jnp.where(odd, first, second)


def row_of(tile, index):
    return jnp.broadcast_to(tile[index : index + 1, :], tile.shape)


def eliminate(panel, offset):
    groups = BLOCK // SUB
    sub_iota = lax.broadcasted_iota(jnp.int32, (SUB, LANES), 0)
    scales = [jnp.zeros((SUB, LANES), jnp.float32) for _ in range(groups)]
    for begin in range(0, BLOCK, STEP):
        columns = [
            [
                jnp.broadcast_to(panel[0][g][:, offset + j : offset + j + 1], (SUB, LANES))
                if g >= begin // SUB
                else None
                for g in range(groups)
            ]
            for j in range(begin, begin + STEP)
        ]
        for p in range(begin, begin + STEP):
            home, line = divmod(p, SUB)
            column = columns[p - begin]
            pivot = row_of(column[home], line)
            inverse = 1.0 / pivot
            scales[home] = jnp.where(sub_iota == line, lax.rsqrt(pivot), scales[home])
            below = list(column)
            below[home] = jnp.where(sub_iota > line, column[home], 0.0)
            last = home + 1 if line == SUB - 1 else home
            for j in range(p + 1, begin + STEP):
                lanes, first = columns[j - begin], j // SUB
                lead = row_of(column[first], j % SUB) * inverse
                for g in range(max(first, last), groups):
                    lanes[g] = lanes[g] - below[g] * lead
            for lanes in panel:
                lead = row_of(lanes[home], line) * inverse
                for g in range(last, groups):
                    lanes[g] = lanes[g] - below[g] * lead
    return [[tile * scale for tile, scale in zip(lanes, scales)] for lanes in panel]


def factor_kernel(mine_ref, other_ref, high_ref, rest_ref, factor_out_ref, directions_ref, *scratch):
    factor_ref, out_ref, a_ref, w_ref, pack_ref, factor_sem, out_sem = scratch
    size = factor_ref.shape[0]
    tiles = size // LANES
    half = mine_ref.shape[0]
    odd = lax.axis_index("cols") % 2 == 1
    pack_ref[pl.ds(0, half), :] = jnp.where(odd, other_ref[...], mine_ref[...])
    pack_ref[pl.ds(half, half), :] = jnp.where(odd, mine_ref[...], other_ref[...])
    pairs, blocks = pack_layout(tiles)
    down, across = square_iota(0), square_iota(1)

    def square(tile):
        return pl.ds(tile * LANES, LANES), pl.ds(tile * LANES, LANES)

    for first, at, line in pairs:
        folded = pack_ref[pl.ds(at, LANES), :]
        turned = folded.T
        a_ref[square(first)] = jnp.where(down <= across, folded, turned)
        diagonal = jnp.broadcast_to(pack_ref[pl.ds(line, 1), :], (LANES, LANES))
        value = jnp.where(down > across, folded, turned)
        a_ref[square(first + 1)] = jnp.where(down == across, diagonal, value)
    for row, col, at in blocks:
        a_ref[pl.ds(row * LANES, LANES), pl.ds(col * LANES, LANES)] = pack_ref[pl.ds(at, LANES), :]
    rows_iota = lax.broadcasted_iota(jnp.int32, (size, size), 0)
    cols_iota = lax.broadcasted_iota(jnp.int32, (size, size), 1)
    w_ref[...] = jnp.where(rows_iota == cols_iota, 1.0, 0.0)

    def row_copies(row):
        rows = pl.ds(row * LANES, LANES)
        return (
            pltpu.make_async_copy(factor_ref.at[rows, :], factor_out_ref.at[rows, :], factor_sem.at[row]),
            pltpu.make_async_copy(out_ref.at[rows, :], directions_ref.at[rows, :], out_sem.at[row]),
        )

    def update_rest(places, panel, a_tiles, after):
        parts = [wide_split(value) for value in panel]
        left = [jnp.concatenate([a, a, b], axis=0) for a, b in parts[: len(a_tiles)]]
        right = [jnp.concatenate([a, b, a], axis=0) for a, b in parts]
        for row_tile in a_tiles:
            skip = max(after - row_tile * LANES, 0)
            if skip == LANES:
                continue
            rows = pl.ds(row_tile * LANES + skip, LANES - skip)
            for (ref, t), value in zip(places, right):
                if ref is a_ref and t < row_tile:
                    continue
                update = tn_dot(left[row_tile - a_tiles[0]], value)
                lanes = pl.ds(t * LANES, LANES)
                ref[rows, lanes] = ref[rows, lanes] - update[skip:, :]

    def emit(row):
        rows = pl.ds(row * LANES, LANES)
        for col in range(tiles):
            into = (rows, pl.ds(col * LANES, LANES))
            if row < col:
                factor_ref[into] = jnp.zeros((LANES, LANES), jnp.float32)
                continue
            block = a_ref[pl.ds(col * LANES, LANES), rows].T
            factor_ref[into] = jnp.where(down >= across, block, 0.0) if row == col else block
        depth, chunk = (row + 1) * LANES, 256
        high, rest = wide_split(w_ref[rows, pl.ds(0, depth)])
        for start in range(0, out_ref.shape[1], chunk):
            cols = pl.ds(start, chunk)
            right_high, right_rest = high_ref[pl.ds(0, depth), cols], rest_ref[pl.ds(0, depth), cols]
            value = jnp.dot(high, right_high, preferred_element_type=jnp.float32)
            value += jnp.dot(high, right_rest, preferred_element_type=jnp.float32)
            value += jnp.dot(rest, right_high, preferred_element_type=jnp.float32)
            out_ref[rows, cols] = value.astype(jnp.bfloat16)

    done_tiles, started = [], 0
    for base in range(0, size, BLOCK):
        tile, offset = divmod(base, LANES)
        a_tiles, w_tiles = range(tile, tiles), range(tile + 1)
        places = [(a_ref, t) for t in a_tiles] + [(w_ref, t) for t in w_tiles]
        panel = [
            [ref[pl.ds(base + g, SUB), pl.ds(t * LANES, LANES)] for g in range(0, BLOCK, SUB)] for ref, t in places
        ]
        panel = [jnp.concatenate(lanes, axis=0) for lanes in eliminate(panel, offset)]
        for (ref, t), value in zip(places, panel):
            ref[pl.ds(base, BLOCK), pl.ds(t * LANES, LANES)] = value
        after = base + BLOCK
        update_rest(places, panel, a_tiles, after)
        if started < len(done_tiles):
            for copy in row_copies(done_tiles[started]):
                copy.start()
            started += 1
        if after % LANES == 0:
            emit(tile)
            done_tiles.append(tile)
    for row in done_tiles[started:]:
        for copy in row_copies(row):
            copy.start()
    for row in done_tiles:
        for copy in row_copies(row):
            copy.wait()


def call(kernel, outs, scratch, flops, grant, whole=0, stay=False):
    vmem = pl.BlockSpec(memory_space=pltpu.VMEM)
    hbm = pl.BlockSpec(memory_space=pltpu.HBM)

    def run(*args):
        size = sum(math.prod(x.shape) * x.dtype.itemsize for x in (*args, *outs))
        args = [pltpu.with_memory_space_constraint(x, pltpu.HBM) for x in args[:whole]] + list(args[whole:])
        return pl.pallas_call(
            kernel,
            out_shape=outs,
            in_specs=[hbm] * whole + [vmem] * (len(args) - whole),
            out_specs=[hbm if stay else vmem] * len(outs),
            scratch_shapes=scratch,
            compiler_params=pltpu.CompilerParams(vmem_limit_bytes=grant << 20),
            cost_estimate=pl.CostEstimate(flops=flops, bytes_accessed=size, transcendentals=0),
        )(*args)

    return run


def shape(dtype, *dims):
    return jax.ShapeDtypeStruct(dims, dtype)


def compute(basis_cols, snapshots):
    snaps, row_points = snapshots.shape
    modes = basis_cols.shape[1]
    row_count, columns = lax.axis_size("rows"), lax.axis_size("cols")
    total_points = row_points * row_count
    points = row_points // columns
    quarter = snaps // 4
    bf16, f32 = jnp.bfloat16, jnp.float32

    row_bits = bits(row_count, columns)
    orders = list(zip(row_bits, row_bits[1:] + row_bits[:1]))
    first, second = orders[0], orders[1]
    both = tuple(a ^ b for a, b in zip(first, second))
    quad = quad_index(first, second)

    slab, piece = shape(bf16, points, modes), shape(f32, quarter, modes)
    slab_scratch, span_scratch = pltpu.VMEM((points, modes), bf16), pltpu.VMEM((snaps, points), bf16)
    semaphores = pltpu.SemaphoreType.DMA((columns,))
    kept, one, two, three, *slabs = call(
        functools.partial(project_kernel, first, second),
        (piece,) * 4 + (slab,) * (columns - 1),
        [slab_scratch] + [span_scratch] * columns + [pltpu.VMEM((snaps, modes), f32), semaphores, semaphores],
        2 * snaps * row_points * modes,
        12,
        2,
    )(basis_cols, snapshots)
    arrived_slabs = [swap(slabs[offset - 1], (offset,) * 2) for offset in range(2, columns)]
    one, two, three = swap(one, first), swap(two, second), swap(three, both)
    near_slab = swap(slabs[0], (1, 1))
    kept = (kept + one) + (two + three)
    for step in orders[2:]:
        kept = kept + swap(kept, step)
    low = (kept * (math.sqrt(RANK) / total_points)).astype(bf16)
    found = (low, swap(low, first), swap(low, second), swap(low, both))
    low = jnp.concatenate([lax.select_n(quad ^ at, *found) for at in range(4)], 0)
    lows = {0: low}
    for offset in range(2, columns, 2):
        lows[offset] = swap(low, (offset, offset))
    for offset in range(0, columns, 2):
        lows[offset + 1] = swap(lows[offset], (1, 1))

    begun, coefficients = call(
        recon_kernel,
        (shape(f32, snaps, points), shape(f32, modes, snaps)),
        [slab_scratch, span_scratch, semaphores, semaphores],
        4 * snaps * points * modes,
        8,
        2,
    )(basis_cols, snapshots, lows[0], lows[1], near_slab)
    packed = packed_rows(snaps // LANES)
    part = shape(f32, packed // 2, LANES)
    wide = shape(bf16, snaps, points)
    high, rest, keep, send = call(
        functools.partial(residual_kernel, total_points),
        (wide, wide, part, part),
        [pltpu.VMEM((packed, LANES), f32)],
        2 * snaps * points * (modes * (columns - 2) + 3 * snaps),
        16,
    )(*[lows[offset] for offset in range(2, columns)], *arrived_slabs, begun)
    keep = keep + swap(send, (1, 1))
    for masks in zip(*exchange_rounds(bits(columns // 2, 2) + row_bits)):
        if masks[0][1] == 0:
            keep = keep + swap(keep, [mask[0] for mask in masks])
            continue
        far = swap(keep, [mask[1] for mask in masks])
        diagonal = swap(keep, [mask[0] ^ mask[1] for mask in masks])
        keep = (keep + swap(keep, [mask[0] for mask in masks])) + (far + diagonal)
    rest_of_gram = swap(keep, (1, 1))
    factor, directions = call(
        factor_kernel,
        (shape(f32, snaps, snaps), wide),
        [pltpu.VMEM((snaps, snaps), f32), span_scratch]
        + [pltpu.VMEM((snaps, snaps), f32)] * 2
        + [pltpu.VMEM((packed, LANES), f32)]
        + [pltpu.SemaphoreType.DMA((snaps // LANES,))] * 2,
        6 * snaps * snaps * points,
        16,
        stay=True,
    )(keep, rest_of_gram, high, rest)
    return (coefficients, factor, directions)


def solution(mesh):
    placed = (P("rows", "cols"), P(None, "rows"))
    return jax.shard_map(
        compute,
        mesh=mesh,
        in_specs=placed,
        out_specs=(P("cols", None), P(), P(None, ("rows", "cols"))),
        check_vma=False,
    )
```

```python
import functools
import math

import jax
import jax.numpy as jnp
from jax import lax
from jax.experimental import pallas as pl
from jax.experimental.pallas import tpu as pltpu
from jax.sharding import PartitionSpec as P


RANK = 1024
LANES = 128
BLOCK = 32
STEP = 16
SUB = 8


def swap(value, masks):
    count = lax.axis_size("rows") * lax.axis_size("cols")
    return lax.ppermute(value, ("rows", "cols"), [(i, i ^ masks[i % 2]) for i in range(count)])


def bits(count, step=1):
    found = []
    while count > 1:
        found.append(step)
        step, count = 2 * step, count // 2
    return found


def exchange_rounds(masks):
    rounds = [(masks[at], masks[at + 1] if at + 1 < len(masks) else 0) for at in range(0, len(masks), 2)]
    paired = [pair for pair in rounds if pair[1]]
    single = [pair for pair in rounds if not pair[1]]
    return paired + single, paired[::-1] + single


def wide_split(value):
    high = value.astype(jnp.bfloat16)
    return high, (value - high.astype(jnp.float32)).astype(jnp.bfloat16)


def nt_dot(left, right):
    return lax.dot_general(left, right, (((1,), (1,)), ((), ())), preferred_element_type=jnp.float32)


def tn_dot(left, right):
    return lax.dot_general(left, right, (((0,), (0,)), ((), ())), preferred_element_type=jnp.float32)


def slab_copies(whole_ref, into_refs, sem_ref, first, by_rows):
    copies = []
    for index, into_ref in enumerate(into_refs):
        size = into_ref.shape[0 if by_rows else 1]
        start = pl.multiple_of((lax.axis_index("cols") ^ (first + index)) * size, size)
        span = whole_ref.at[pl.ds(start, size), :] if by_rows else whole_ref.at[:, pl.ds(start, size)]
        copies.append(pltpu.make_async_copy(span, into_ref, sem_ref.at[index]))
    return copies


def quad_index(first, second):
    column = lax.axis_index("cols")
    flat = lax.axis_index("rows") * lax.axis_size("cols") + column
    low, high = (flat // jnp.where(column % 2 == 0, *masks) % 2 for masks in (first, second))
    return (low + 2 * high).astype(jnp.int32)


def project_kernel(first, second, basis_ref, snaps_ref, *refs):
    count = (len(refs) - 7) // 2
    piece_refs, slab_refs = refs[:4], (refs[3 + count],) + refs[4 : 3 + count]
    part_refs, total_ref, basis_sem, snaps_sem = refs[4 + count : 4 + 2 * count], refs[-3], refs[-2], refs[-1]
    basis_copies = slab_copies(basis_ref, slab_refs, basis_sem, 0, True)
    snaps_copies = slab_copies(snaps_ref, part_refs, snaps_sem, 0, False)
    for pair in zip(basis_copies, snaps_copies):
        for copy in pair:
            copy.start()
    total = None
    for offset in range(count):
        basis_copies[offset].wait()
        snaps_copies[offset].wait()
        value = jnp.dot(part_refs[offset][...], slab_refs[offset][...], preferred_element_type=jnp.float32)
        total = value if total is None else total + value
    total_ref[...] = total
    rows = piece_refs[0].shape[0]
    quad = quad_index(first, second)
    for offset, piece_ref in enumerate(piece_refs):
        start = pl.multiple_of((quad ^ offset) * rows, rows)
        piece_ref[...] = total_ref[pl.ds(start, rows), :]


def recon_kernel(basis_ref, snaps_ref, low_ref, near_low_ref, near_ref, base_ref, coefficients_ref, *scratch):
    own_ref, span_ref, basis_sem, snaps_sem = scratch
    (basis_copy,) = slab_copies(basis_ref, (own_ref,), basis_sem, 0, True)
    (snaps_copy,) = slab_copies(snaps_ref, (span_ref,), snaps_sem, 0, False)
    basis_copy.start()
    snaps_copy.start()
    coefficients_ref[...] = low_ref[...].astype(jnp.float32).T
    basis_copy.wait()
    snaps_copy.wait()
    chunk = 256
    for start in range(0, base_ref.shape[1], chunk):
        cols = slice(start, start + chunk)
        recon = nt_dot(low_ref[...], own_ref[cols, :]) + nt_dot(near_low_ref[...], near_ref[cols, :])
        base_ref[:, cols] = span_ref[:, cols].astype(jnp.float32) - recon * (1.0 / math.sqrt(RANK))


def packed_rows(tiles):
    return tiles // 2 * (LANES + 2 * SUB) + tiles * (tiles - 1) // 2 * LANES


def pack_layout(tiles):
    at, pairs, blocks = 0, [], []
    for first in range(0, tiles, 2):
        pairs.append((first, at, at + LANES))
        at += LANES + 2 * SUB
    for row in range(tiles):
        for col in range(row + 1, tiles):
            blocks.append((row, col, at))
            at += LANES
    return pairs, blocks


def square_iota(dim):
    return lax.broadcasted_iota(jnp.int32, (LANES, LANES), dim)


def residual_kernel(total_points, *refs):
    count = (len(refs) - 6) // 2
    low_refs, basis_refs = refs[:count], refs[count : 2 * count]
    base_ref, high_ref, rest_ref, keep_ref, send_ref, pack_ref = refs[2 * count :]
    snaps, points = base_ref.shape
    chunk = 256
    for start in range(0, points, chunk):
        cols = slice(start, start + chunk)
        recon = nt_dot(low_refs[0][...], basis_refs[0][cols, :])
        for low_ref, basis_ref in zip(low_refs[1:], basis_refs[1:]):
            recon += nt_dot(low_ref[...], basis_ref[cols, :])
        high, rest = wide_split(base_ref[:, cols] - recon * (1.0 / math.sqrt(RANK)))
        high_ref[:, cols] = high
        rest_ref[:, cols] = rest
    scale = 1.0 / total_points

    high, rest = high_ref[...], rest_ref[...]
    gram = (nt_dot(high, high) + (nt_dot(high, rest) + nt_dot(rest, high))) * scale

    def block(row, col):
        return gram[row * LANES : (row + 1) * LANES, col * LANES : (col + 1) * LANES]

    pairs, blocks = pack_layout(snaps // LANES)
    down, across = square_iota(0), square_iota(1)
    for first, at, line in pairs:
        upper, lower = block(first, first), block(first + 1, first + 1)
        pack_ref[pl.ds(at, LANES), :] = jnp.where(down <= across, upper, lower)
        diagonal = jnp.sum(jnp.where(down == across, lower, 0.0), axis=0, keepdims=True)
        pack_ref[pl.ds(line, 2 * SUB), :] = jnp.broadcast_to(diagonal, (2 * SUB, LANES))
    for row, col, at in blocks:
        pack_ref[pl.ds(at, LANES), :] = block(row, col)
    half = pack_ref.shape[0] // 2
    odd = lax.axis_index("cols") % 2 == 1
    first, second = pack_ref[pl.ds(0, half), :], pack_ref[pl.ds(half, half), :]
    keep_ref[...] = jnp.where(odd, second, first)
    send_ref[...] = jnp.where(odd, first, second)


def row_of(tile, index):
    return jnp.broadcast_to(tile[index : index + 1, :], tile.shape)


def eliminate(panel, offset):
    groups = BLOCK // SUB
    sub_iota = lax.broadcasted_iota(jnp.int32, (SUB, LANES), 0)
    scales = [jnp.zeros((SUB, LANES), jnp.float32) for _ in range(groups)]
    for begin in range(0, BLOCK, STEP):
        columns = [
            [
                jnp.broadcast_to(panel[0][g][:, offset + j : offset + j + 1], (SUB, LANES))
                if g >= begin // SUB
                else None
                for g in range(groups)
            ]
            for j in range(begin, begin + STEP)
        ]
        for p in range(begin, begin + STEP, 2):
            home, line = divmod(p, SUB)
            left, right = columns[p - begin], columns[p + 1 - begin]
            pivot, cross = row_of(left[home], line), row_of(left[home], line + 1)
            both = pivot * row_of(right[home], line + 1) - cross * cross
            inverse = 1.0 / pivot
            second = pivot * (1.0 / both)
            ratio = cross * inverse
            scales[home] = jnp.where(sub_iota == line, lax.rsqrt(pivot), scales[home])
            scales[home] = jnp.where(sub_iota == line + 1, lax.rsqrt(both * inverse), scales[home])
            right = [None if tile is None else tile - ratio * left[g] for g, tile in enumerate(right)]
            below, under = list(left), list(right)
            below[home] = jnp.where(sub_iota > line, left[home], 0.0)
            under[home] = jnp.where(sub_iota > line + 1, right[home], 0.0)
            last = home + 1 if line + 2 == SUB else home
            for j in range(p + 2, begin + STEP):
                lanes, first = columns[j - begin], j // SUB
                lead, next_lead = row_of(left[first], j % SUB) * inverse, row_of(right[first], j % SUB) * second
                for g in range(max(first, last), groups):
                    lanes[g] = (lanes[g] - below[g] * lead) - under[g] * next_lead
            for lanes in panel:
                top = row_of(lanes[home], line)
                lead, next_lead = top * inverse, (row_of(lanes[home], line + 1) - ratio * top) * second
                for g in range(home, groups):
                    lanes[g] = lanes[g] - below[g] * lead
                    if g >= last:
                        lanes[g] = lanes[g] - under[g] * next_lead
    return [[tile * scale for tile, scale in zip(lanes, scales)] for lanes in panel]


def factor_kernel(mine_ref, other_ref, high_ref, rest_ref, factor_out_ref, directions_ref, *scratch):
    factor_ref, out_ref, a_ref, w_ref, pack_ref, factor_sem, out_sem = scratch
    size = factor_ref.shape[0]
    tiles = size // LANES
    half = mine_ref.shape[0]
    odd = lax.axis_index("cols") % 2 == 1
    pack_ref[pl.ds(0, half), :] = jnp.where(odd, other_ref[...], mine_ref[...])
    pack_ref[pl.ds(half, half), :] = jnp.where(odd, mine_ref[...], other_ref[...])
    pairs, blocks = pack_layout(tiles)
    down, across = square_iota(0), square_iota(1)

    def square(tile):
        return pl.ds(tile * LANES, LANES), pl.ds(tile * LANES, LANES)

    diagonals = {}
    for first, at, line in pairs:
        inner = jnp.where(down == across, pack_ref[pl.ds(at, LANES), :], 0.0)
        diagonals[first] = jnp.sum(inner, axis=0, keepdims=True)
        diagonals[first + 1] = pack_ref[pl.ds(line, 1), :]
    rows_by = [jnp.broadcast_to(lax.rsqrt(diagonals[tile]), (LANES, LANES)) for tile in range(tiles)]
    roots = [diagonals[tile] * lax.rsqrt(diagonals[tile]) for tile in range(tiles)]
    down_by = [value.T for value in rows_by]

    for first, at, line in pairs:
        folded = pack_ref[pl.ds(at, LANES), :]
        turned = folded.T
        value = jnp.where(down <= across, folded, turned)
        a_ref[square(first)] = value * down_by[first] * rows_by[first]
        diagonal = jnp.broadcast_to(diagonals[first + 1], (LANES, LANES))
        value = jnp.where(down == across, diagonal, jnp.where(down > across, folded, turned))
        a_ref[square(first + 1)] = value * down_by[first + 1] * rows_by[first + 1]
    for row, col, at in blocks:
        value = pack_ref[pl.ds(at, LANES), :] * down_by[row] * rows_by[col]
        a_ref[pl.ds(row * LANES, LANES), pl.ds(col * LANES, LANES)] = value
    w_ref[...] = jnp.zeros((size, size), jnp.float32)
    for tile in range(tiles):
        w_ref[square(tile)] = jnp.where(down == across, rows_by[tile], 0.0)

    def row_copies(row):
        rows = pl.ds(row * LANES, LANES)
        return (
            pltpu.make_async_copy(factor_ref.at[rows, :], factor_out_ref.at[rows, :], factor_sem.at[row]),
            pltpu.make_async_copy(out_ref.at[rows, :], directions_ref.at[rows, :], out_sem.at[row]),
        )

    def update_rest(places, panel, a_tiles, after):
        parts = [wide_split(value) for value in panel]
        left = [jnp.concatenate([a, a, b], axis=0) for a, b in parts[: len(a_tiles)]]
        right = [jnp.concatenate([a, b, a], axis=0) for a, b in parts]
        for row_tile in a_tiles:
            skip = max(after - row_tile * LANES, 0)
            if skip == LANES:
                continue
            rows = pl.ds(row_tile * LANES + skip, LANES - skip)
            used = [(place, value) for place, value in zip(places, right) if place[0] is w_ref or place[1] >= row_tile]
            wide = tn_dot(left[row_tile - a_tiles[0]], jnp.concatenate([value for _, value in used], axis=1))
            for index, ((ref, t), _) in enumerate(used):
                lanes = pl.ds(t * LANES, LANES)
                ref[rows, lanes] = ref[rows, lanes] - wide[skip:, index * LANES : (index + 1) * LANES]

    def emit(row):
        rows = pl.ds(row * LANES, LANES)
        for col in range(tiles):
            into = (rows, pl.ds(col * LANES, LANES))
            if row < col:
                factor_ref[into] = jnp.zeros((LANES, LANES), jnp.float32)
                continue
            block = (a_ref[pl.ds(col * LANES, LANES), rows] * roots[row]).T
            factor_ref[into] = jnp.where(down >= across, block, 0.0) if row == col else block
        depth, chunk = (row + 1) * LANES, 256
        high, rest = wide_split(w_ref[rows, pl.ds(0, depth)])
        for start in range(0, out_ref.shape[1], chunk):
            cols = pl.ds(start, chunk)
            right_high, right_rest = high_ref[pl.ds(0, depth), cols], rest_ref[pl.ds(0, depth), cols]
            value = jnp.dot(high, right_high, preferred_element_type=jnp.float32)
            value += jnp.dot(high, right_rest, preferred_element_type=jnp.float32)
            value += jnp.dot(rest, right_high, preferred_element_type=jnp.float32)
            out_ref[rows, cols] = value.astype(jnp.bfloat16)

    done_tiles, started = [], 0
    for base in range(0, size, BLOCK):
        tile, offset = divmod(base, LANES)
        a_tiles, w_tiles = range(tile, tiles), range(tile + 1)
        places = [(a_ref, t) for t in a_tiles] + [(w_ref, t) for t in w_tiles]
        panel = [
            [ref[pl.ds(base + g, SUB), pl.ds(t * LANES, LANES)] for g in range(0, BLOCK, SUB)] for ref, t in places
        ]
        panel = [jnp.concatenate(lanes, axis=0) for lanes in eliminate(panel, offset)]
        for (ref, t), value in zip(places, panel):
            ref[pl.ds(base, BLOCK), pl.ds(t * LANES, LANES)] = value
        after = base + BLOCK
        update_rest(places, panel, a_tiles, after)
        if started < len(done_tiles):
            for copy in row_copies(done_tiles[started]):
                copy.start()
            started += 1
        if after % LANES == 0:
            emit(tile)
            done_tiles.append(tile)
    for row in done_tiles[started:]:
        for copy in row_copies(row):
            copy.start()
    for row in done_tiles:
        for copy in row_copies(row):
            copy.wait()


def call(kernel, outs, scratch, flops, grant, whole=0, stay=False):
    vmem = pl.BlockSpec(memory_space=pltpu.VMEM)
    hbm = pl.BlockSpec(memory_space=pltpu.HBM)

    def run(*args):
        size = sum(math.prod(x.shape) * x.dtype.itemsize for x in (*args, *outs))
        args = [pltpu.with_memory_space_constraint(x, pltpu.HBM) for x in args[:whole]] + list(args[whole:])
        return pl.pallas_call(
            kernel,
            out_shape=outs,
            in_specs=[hbm] * whole + [vmem] * (len(args) - whole),
            out_specs=[hbm if stay else vmem] * len(outs),
            scratch_shapes=scratch,
            compiler_params=pltpu.CompilerParams(vmem_limit_bytes=grant << 20),
            cost_estimate=pl.CostEstimate(flops=flops, bytes_accessed=size, transcendentals=0),
        )(*args)

    return run


def shape(dtype, *dims):
    return jax.ShapeDtypeStruct(dims, dtype)


def compute(basis_cols, snapshots):
    snaps, row_points = snapshots.shape
    modes = basis_cols.shape[1]
    row_count, columns = lax.axis_size("rows"), lax.axis_size("cols")
    total_points = row_points * row_count
    points = row_points // columns
    quarter = snaps // 4
    bf16, f32 = jnp.bfloat16, jnp.float32

    row_bits = bits(row_count, columns)
    orders = list(zip(row_bits, row_bits[1:] + row_bits[:1]))
    first, second = orders[0], orders[1]
    both = tuple(a ^ b for a, b in zip(first, second))
    quad = quad_index(first, second)

    slab, piece = shape(bf16, points, modes), shape(f32, quarter, modes)
    slab_scratch, span_scratch = pltpu.VMEM((points, modes), bf16), pltpu.VMEM((snaps, points), bf16)
    semaphores = pltpu.SemaphoreType.DMA((columns,))
    kept, one, two, three, *slabs = call(
        functools.partial(project_kernel, first, second),
        (piece,) * 4 + (slab,) * (columns - 1),
        [slab_scratch] + [span_scratch] * columns + [pltpu.VMEM((snaps, modes), f32), semaphores, semaphores],
        2 * snaps * row_points * modes,
        12,
        2,
    )(basis_cols, snapshots)
    arrived_slabs = [swap(slabs[offset - 1], (offset,) * 2) for offset in range(2, columns)]
    one, two, three = swap(one, first), swap(two, second), swap(three, both)
    near_slab = swap(slabs[0], (1, 1))
    kept = (kept + one) + (two + three)
    for step in orders[2:]:
        kept = kept + swap(kept, step)
    low = (kept * (math.sqrt(RANK) / total_points)).astype(bf16)
    found = (low, swap(low, first), swap(low, second), swap(low, both))
    low = jnp.concatenate([lax.select_n(quad ^ at, *found) for at in range(4)], 0)
    lows = {0: low}
    for offset in range(2, columns, 2):
        lows[offset] = swap(low, (offset, offset))
    for offset in range(0, columns, 2):
        lows[offset + 1] = swap(lows[offset], (1, 1))

    begun, coefficients = call(
        recon_kernel,
        (shape(f32, snaps, points), shape(f32, modes, snaps)),
        [slab_scratch, span_scratch, semaphores, semaphores],
        4 * snaps * points * modes,
        8,
        2,
    )(basis_cols, snapshots, lows[0], lows[1], near_slab)
    packed = packed_rows(snaps // LANES)
    part = shape(f32, packed // 2, LANES)
    wide = shape(bf16, snaps, points)
    high, rest, keep, send = call(
        functools.partial(residual_kernel, total_points),
        (wide, wide, part, part),
        [pltpu.VMEM((packed, LANES), f32)],
        2 * snaps * points * (modes * (columns - 2) + 3 * snaps),
        16,
    )(*[lows[offset] for offset in range(2, columns)], *arrived_slabs, begun)
    keep = keep + swap(send, (1, 1))
    for masks in zip(*exchange_rounds(bits(columns // 2, 2) + row_bits)):
        if masks[0][1] == 0:
            keep = keep + swap(keep, [mask[0] for mask in masks])
            continue
        far = swap(keep, [mask[1] for mask in masks])
        diagonal = swap(keep, [mask[0] ^ mask[1] for mask in masks])
        keep = (keep + swap(keep, [mask[0] for mask in masks])) + (far + diagonal)
    rest_of_gram = swap(keep, (1, 1))
    factor, directions = call(
        factor_kernel,
        (shape(f32, snaps, snaps), wide),
        [pltpu.VMEM((snaps, snaps), f32), span_scratch]
        + [pltpu.VMEM((snaps, snaps), f32)] * 2
        + [pltpu.VMEM((packed, LANES), f32)]
        + [pltpu.SemaphoreType.DMA((snaps // LANES,))] * 2,
        6 * snaps * snaps * points,
        16,
        stay=True,
    )(keep, rest_of_gram, high, rest)
    return (coefficients, factor, directions)


def solution(mesh):
    placed = (P("rows", "cols"), P(None, "rows"))
    return jax.shard_map(
        compute,
        mesh=mesh,
        in_specs=placed,
        out_specs=(P("cols", None), P(), P(None, ("rows", "cols"))),
        check_vma=False,
    )
```

```python
import functools
import math

import jax
import jax.numpy as jnp
from jax import lax
from jax.experimental import pallas as pl
from jax.experimental.pallas import tpu as pltpu
from jax.sharding import PartitionSpec as P


RANK = 1024
LANES = 128
BLOCK = 32
STEP = 16
SUB = 8


def swap(value, masks):
    count = lax.axis_size("rows") * lax.axis_size("cols")
    return lax.ppermute(value, ("rows", "cols"), [(i, i ^ masks[i % 2]) for i in range(count)])


def bits(count, step=1):
    found = []
    while count > 1:
        found.append(step)
        step, count = 2 * step, count // 2
    return found


def exchange_rounds(masks):
    rounds = [(masks[at], masks[at + 1] if at + 1 < len(masks) else 0) for at in range(0, len(masks), 2)]
    paired = [pair for pair in rounds if pair[1]]
    single = [pair for pair in rounds if not pair[1]]
    return paired + single, paired[::-1] + single


def wide_split(value):
    high = value.astype(jnp.bfloat16)
    return high, (value - high.astype(jnp.float32)).astype(jnp.bfloat16)


def nt_dot(left, right):
    return lax.dot_general(left, right, (((1,), (1,)), ((), ())), preferred_element_type=jnp.float32)


def tn_dot(left, right):
    return lax.dot_general(left, right, (((0,), (0,)), ((), ())), preferred_element_type=jnp.float32)


def slab_copies(whole_ref, into_refs, sem_ref, first, by_rows):
    copies = []
    for index, into_ref in enumerate(into_refs):
        size = into_ref.shape[0 if by_rows else 1]
        start = pl.multiple_of((lax.axis_index("cols") ^ (first + index)) * size, size)
        span = whole_ref.at[pl.ds(start, size), :] if by_rows else whole_ref.at[:, pl.ds(start, size)]
        copies.append(pltpu.make_async_copy(span, into_ref, sem_ref.at[index]))
    return copies


def quad_index(first, second):
    column = lax.axis_index("cols")
    flat = lax.axis_index("rows") * lax.axis_size("cols") + column
    low, high = (flat // jnp.where(column % 2 == 0, *masks) % 2 for masks in (first, second))
    return (low + 2 * high).astype(jnp.int32)


def project_kernel(first, second, basis_ref, snaps_ref, *refs):
    count = (len(refs) - 7) // 2
    piece_refs, slab_refs = refs[:4], (refs[3 + count],) + refs[4 : 3 + count]
    part_refs, total_ref, basis_sem, snaps_sem = refs[4 + count : 4 + 2 * count], refs[-3], refs[-2], refs[-1]
    basis_copies = slab_copies(basis_ref, slab_refs, basis_sem, 0, True)
    snaps_copies = slab_copies(snaps_ref, part_refs, snaps_sem, 0, False)
    for pair in zip(basis_copies, snaps_copies):
        for copy in pair:
            copy.start()
    total = None
    for offset in range(count):
        basis_copies[offset].wait()
        snaps_copies[offset].wait()
        value = jnp.dot(part_refs[offset][...], slab_refs[offset][...], preferred_element_type=jnp.float32)
        total = value if total is None else total + value
    total_ref[...] = total
    rows = piece_refs[0].shape[0]
    quad = quad_index(first, second)
    for offset, piece_ref in enumerate(piece_refs):
        start = pl.multiple_of((quad ^ offset) * rows, rows)
        piece_ref[...] = total_ref[pl.ds(start, rows), :]


def recon_kernel(basis_ref, snaps_ref, low_ref, near_low_ref, near_ref, base_ref, coefficients_ref, *scratch):
    own_ref, span_ref, basis_sem, snaps_sem = scratch
    (basis_copy,) = slab_copies(basis_ref, (own_ref,), basis_sem, 0, True)
    (snaps_copy,) = slab_copies(snaps_ref, (span_ref,), snaps_sem, 0, False)
    basis_copy.start()
    snaps_copy.start()
    coefficients_ref[...] = low_ref[...].astype(jnp.float32).T
    basis_copy.wait()
    snaps_copy.wait()
    chunk = 256
    for start in range(0, base_ref.shape[1], chunk):
        cols = slice(start, start + chunk)
        recon = nt_dot(low_ref[...], own_ref[cols, :]) + nt_dot(near_low_ref[...], near_ref[cols, :])
        base_ref[:, cols] = span_ref[:, cols].astype(jnp.float32) - recon * (1.0 / math.sqrt(RANK))


def packed_rows(tiles):
    return tiles // 2 * (LANES + 2 * SUB) + tiles * (tiles - 1) // 2 * LANES


def pack_layout(tiles):
    at, pairs, blocks = 0, [], []
    for first in range(0, tiles, 2):
        pairs.append((first, at, at + LANES))
        at += LANES + 2 * SUB
    for row in range(tiles):
        for col in range(row + 1, tiles):
            blocks.append((row, col, at))
            at += LANES
    return pairs, blocks


def square_iota(dim):
    return lax.broadcasted_iota(jnp.int32, (LANES, LANES), dim)


def residual_kernel(total_points, *refs):
    count = (len(refs) - 6) // 2
    low_refs, basis_refs = refs[:count], refs[count : 2 * count]
    base_ref, high_ref, rest_ref, keep_ref, send_ref, pack_ref = refs[2 * count :]
    snaps, points = base_ref.shape
    chunk = 512
    for start in range(0, points, chunk):
        cols = slice(start, start + chunk)
        recon = nt_dot(low_refs[0][...], basis_refs[0][cols, :])
        for low_ref, basis_ref in zip(low_refs[1:], basis_refs[1:]):
            recon += nt_dot(low_ref[...], basis_ref[cols, :])
        high, rest = wide_split(base_ref[:, cols] - recon * (1.0 / math.sqrt(RANK)))
        high_ref[:, cols] = high
        rest_ref[:, cols] = rest
    scale = 1.0 / total_points

    high, rest = high_ref[...], rest_ref[...]
    gram = (nt_dot(high, high) + (nt_dot(high, rest) + nt_dot(rest, high))) * scale

    def block(row, col):
        return gram[row * LANES : (row + 1) * LANES, col * LANES : (col + 1) * LANES]

    pairs, blocks = pack_layout(snaps // LANES)
    down, across = square_iota(0), square_iota(1)
    for first, at, line in pairs:
        upper, lower = block(first, first), block(first + 1, first + 1)
        pack_ref[pl.ds(at, LANES), :] = jnp.where(down <= across, upper, lower)
        diagonal = jnp.sum(jnp.where(down == across, lower, 0.0), axis=0, keepdims=True)
        pack_ref[pl.ds(line, 2 * SUB), :] = jnp.broadcast_to(diagonal, (2 * SUB, LANES))
    for row, col, at in blocks:
        pack_ref[pl.ds(at, LANES), :] = block(row, col)
    half = pack_ref.shape[0] // 2
    odd = lax.axis_index("cols") % 2 == 1
    first, second = pack_ref[pl.ds(0, half), :], pack_ref[pl.ds(half, half), :]
    keep_ref[...] = jnp.where(odd, second, first)
    send_ref[...] = jnp.where(odd, first, second)


def row_of(tile, index):
    return jnp.broadcast_to(tile[index : index + 1, :], tile.shape)


def eliminate(panel, offset):
    groups = BLOCK // SUB
    sub_iota = lax.broadcasted_iota(jnp.int32, (SUB, LANES), 0)
    scales = [jnp.zeros((SUB, LANES), jnp.float32) for _ in range(groups)]
    for begin in range(0, BLOCK, STEP):
        columns = [
            [
                jnp.broadcast_to(panel[0][g][:, offset + j : offset + j + 1], (SUB, LANES))
                if g >= begin // SUB
                else None
                for g in range(groups)
            ]
            for j in range(begin, begin + STEP)
        ]
        for p in range(begin, begin + STEP, 2):
            home, line = divmod(p, SUB)
            left, right = columns[p - begin], columns[p + 1 - begin]
            pivot, cross = row_of(left[home], line), row_of(left[home], line + 1)
            both = pivot * row_of(right[home], line + 1) - cross * cross
            inverse = 1.0 / pivot
            second = pivot * (1.0 / both)
            ratio = cross * inverse
            scales[home] = jnp.where(sub_iota == line, lax.rsqrt(pivot), scales[home])
            scales[home] = jnp.where(sub_iota == line + 1, lax.rsqrt(both * inverse), scales[home])
            right = [None if tile is None else tile - ratio * left[g] for g, tile in enumerate(right)]
            below, under = list(left), list(right)
            below[home] = jnp.where(sub_iota > line, left[home], 0.0)
            under[home] = jnp.where(sub_iota > line + 1, right[home], 0.0)
            last = home + 1 if line + 2 == SUB else home
            for j in range(p + 2, begin + STEP):
                lanes, first = columns[j - begin], j // SUB
                lead, next_lead = row_of(left[first], j % SUB) * inverse, row_of(right[first], j % SUB) * second
                for g in range(max(first, last), groups):
                    lanes[g] = (lanes[g] - below[g] * lead) - under[g] * next_lead
            for lanes in panel:
                top = row_of(lanes[home], line)
                lead, next_lead = top * inverse, (row_of(lanes[home], line + 1) - ratio * top) * second
                for g in range(home, groups):
                    lanes[g] = lanes[g] - below[g] * lead
                    if g >= last:
                        lanes[g] = lanes[g] - under[g] * next_lead
    return [[tile * scale for tile, scale in zip(lanes, scales)] for lanes in panel]


def factor_kernel(mine_ref, other_ref, high_ref, rest_ref, factor_out_ref, directions_ref, *scratch):
    factor_ref, out_ref, a_ref, w_ref, pack_ref, factor_sem, out_sem = scratch
    size = factor_ref.shape[0]
    tiles = size // LANES
    half = mine_ref.shape[0]
    odd = lax.axis_index("cols") % 2 == 1
    pack_ref[pl.ds(0, half), :] = jnp.where(odd, other_ref[...], mine_ref[...])
    pack_ref[pl.ds(half, half), :] = jnp.where(odd, mine_ref[...], other_ref[...])
    pairs, blocks = pack_layout(tiles)
    down, across = square_iota(0), square_iota(1)

    def square(tile):
        return pl.ds(tile * LANES, LANES), pl.ds(tile * LANES, LANES)

    diagonals = {}
    for first, at, line in pairs:
        inner = jnp.where(down == across, pack_ref[pl.ds(at, LANES), :], 0.0)
        diagonals[first] = jnp.sum(inner, axis=0, keepdims=True)
        diagonals[first + 1] = pack_ref[pl.ds(line, 1), :]
    rows_by = [jnp.broadcast_to(lax.rsqrt(diagonals[tile]), (LANES, LANES)) for tile in range(tiles)]
    roots = [diagonals[tile] * lax.rsqrt(diagonals[tile]) for tile in range(tiles)]
    down_by = [value.T for value in rows_by]

    for first, at, line in pairs:
        folded = pack_ref[pl.ds(at, LANES), :]
        turned = folded.T
        value = jnp.where(down <= across, folded, turned)
        a_ref[square(first)] = value * down_by[first] * rows_by[first]
        diagonal = jnp.broadcast_to(diagonals[first + 1], (LANES, LANES))
        value = jnp.where(down == across, diagonal, jnp.where(down > across, folded, turned))
        a_ref[square(first + 1)] = value * down_by[first + 1] * rows_by[first + 1]
    for row, col, at in blocks:
        value = pack_ref[pl.ds(at, LANES), :] * down_by[row] * rows_by[col]
        a_ref[pl.ds(row * LANES, LANES), pl.ds(col * LANES, LANES)] = value
    w_ref[...] = jnp.zeros((size, size), jnp.float32)
    for tile in range(tiles):
        w_ref[square(tile)] = jnp.where(down == across, rows_by[tile], 0.0)

    def row_copies(row):
        rows = pl.ds(row * LANES, LANES)
        return (
            pltpu.make_async_copy(factor_ref.at[rows, :], factor_out_ref.at[rows, :], factor_sem.at[row]),
            pltpu.make_async_copy(out_ref.at[rows, :], directions_ref.at[rows, :], out_sem.at[row]),
        )

    def update_rest(places, panel, a_tiles, after):
        parts = [wide_split(value) for value in panel]
        left = [jnp.concatenate([a, a, b], axis=0) for a, b in parts[: len(a_tiles)]]
        right = [jnp.concatenate([a, b, a], axis=0) for a, b in parts]
        for row_tile in a_tiles:
            skip = max(after - row_tile * LANES, 0)
            if skip == LANES:
                continue
            rows = pl.ds(row_tile * LANES + skip, LANES - skip)
            for (ref, t), value in zip(places, right):
                if ref is a_ref and t < row_tile:
                    continue
                update = tn_dot(left[row_tile - a_tiles[0]], value)
                lanes = pl.ds(t * LANES, LANES)
                ref[rows, lanes] = ref[rows, lanes] - update[skip:, :]

    def emit(row):
        rows = pl.ds(row * LANES, LANES)
        for col in range(tiles):
            into = (rows, pl.ds(col * LANES, LANES))
            if row < col:
                factor_ref[into] = jnp.zeros((LANES, LANES), jnp.float32)
                continue
            block = (a_ref[pl.ds(col * LANES, LANES), rows] * roots[row]).T
            factor_ref[into] = jnp.where(down >= across, block, 0.0) if row == col else block
        depth, chunk = (row + 1) * LANES, 256
        high, rest = wide_split(w_ref[rows, pl.ds(0, depth)])
        for start in range(0, out_ref.shape[1], chunk):
            cols = pl.ds(start, chunk)
            right_high, right_rest = high_ref[pl.ds(0, depth), cols], rest_ref[pl.ds(0, depth), cols]
            value = jnp.dot(high, right_high, preferred_element_type=jnp.float32)
            value += jnp.dot(high, right_rest, preferred_element_type=jnp.float32)
            value += jnp.dot(rest, right_high, preferred_element_type=jnp.float32)
            out_ref[rows, cols] = value.astype(jnp.bfloat16)

    done_tiles, started = [], 0
    for base in range(0, size, BLOCK):
        tile, offset = divmod(base, LANES)
        a_tiles, w_tiles = range(tile, tiles), range(tile + 1)
        places = [(a_ref, t) for t in a_tiles] + [(w_ref, t) for t in w_tiles]
        panel = [
            [ref[pl.ds(base + g, SUB), pl.ds(t * LANES, LANES)] for g in range(0, BLOCK, SUB)] for ref, t in places
        ]
        panel = [jnp.concatenate(lanes, axis=0) for lanes in eliminate(panel, offset)]
        for (ref, t), value in zip(places, panel):
            ref[pl.ds(base, BLOCK), pl.ds(t * LANES, LANES)] = value
        after = base + BLOCK
        update_rest(places, panel, a_tiles, after)
        if started < len(done_tiles):
            for copy in row_copies(done_tiles[started]):
                copy.start()
            started += 1
        if after % LANES == 0:
            emit(tile)
            done_tiles.append(tile)
    for row in done_tiles[started:]:
        for copy in row_copies(row):
            copy.start()
    for row in done_tiles:
        for copy in row_copies(row):
            copy.wait()


def call(kernel, outs, scratch, flops, grant, whole=0, stay=False):
    vmem = pl.BlockSpec(memory_space=pltpu.VMEM)
    hbm = pl.BlockSpec(memory_space=pltpu.HBM)

    def run(*args):
        size = sum(math.prod(x.shape) * x.dtype.itemsize for x in (*args, *outs))
        args = [pltpu.with_memory_space_constraint(x, pltpu.HBM) for x in args[:whole]] + list(args[whole:])
        return pl.pallas_call(
            kernel,
            out_shape=outs,
            in_specs=[hbm] * whole + [vmem] * (len(args) - whole),
            out_specs=[hbm if stay else vmem] * len(outs),
            scratch_shapes=scratch,
            compiler_params=pltpu.CompilerParams(vmem_limit_bytes=grant << 20),
            cost_estimate=pl.CostEstimate(flops=flops, bytes_accessed=size, transcendentals=0),
        )(*args)

    return run


def shape(dtype, *dims):
    return jax.ShapeDtypeStruct(dims, dtype)


def compute(basis_cols, snapshots):
    snaps, row_points = snapshots.shape
    modes = basis_cols.shape[1]
    row_count, columns = lax.axis_size("rows"), lax.axis_size("cols")
    total_points = row_points * row_count
    points = row_points // columns
    quarter = snaps // 4
    bf16, f32 = jnp.bfloat16, jnp.float32

    row_bits = bits(row_count, columns)
    orders = list(zip(row_bits, row_bits[1:] + row_bits[:1]))
    first, second = orders[0], orders[1]
    both = tuple(a ^ b for a, b in zip(first, second))
    quad = quad_index(first, second)

    slab, piece = shape(bf16, points, modes), shape(f32, quarter, modes)
    slab_scratch, span_scratch = pltpu.VMEM((points, modes), bf16), pltpu.VMEM((snaps, points), bf16)
    semaphores = pltpu.SemaphoreType.DMA((columns,))
    kept, one, two, three, *slabs = call(
        functools.partial(project_kernel, first, second),
        (piece,) * 4 + (slab,) * (columns - 1),
        [slab_scratch] + [span_scratch] * columns + [pltpu.VMEM((snaps, modes), f32), semaphores, semaphores],
        2 * snaps * row_points * modes,
        12,
        2,
    )(basis_cols, snapshots)
    arrived_slabs = [swap(slabs[offset - 1], (offset,) * 2) for offset in range(2, columns)]
    one, two, three = swap(one, first), swap(two, second), swap(three, both)
    near_slab = swap(slabs[0], (1, 1))
    kept = (kept + one) + (two + three)
    for step in orders[2:]:
        kept = kept + swap(kept, step)
    low = (kept * (math.sqrt(RANK) / total_points)).astype(bf16)
    found = (low, swap(low, first), swap(low, second), swap(low, both))
    low = jnp.concatenate([lax.select_n(quad ^ at, *found) for at in range(4)], 0)
    lows = {0: low}
    for offset in range(2, columns, 2):
        lows[offset] = swap(low, (offset, offset))
    for offset in range(0, columns, 2):
        lows[offset + 1] = swap(lows[offset], (1, 1))

    begun, coefficients = call(
        recon_kernel,
        (shape(f32, snaps, points), shape(f32, modes, snaps)),
        [slab_scratch, span_scratch, semaphores, semaphores],
        4 * snaps * points * modes,
        8,
        2,
    )(basis_cols, snapshots, lows[0], lows[1], near_slab)
    packed = packed_rows(snaps // LANES)
    part = shape(f32, packed // 2, LANES)
    wide = shape(bf16, snaps, points)
    high, rest, keep, send = call(
        functools.partial(residual_kernel, total_points),
        (wide, wide, part, part),
        [pltpu.VMEM((packed, LANES), f32)],
        2 * snaps * points * (modes * (columns - 2) + 3 * snaps),
        16,
    )(*[lows[offset] for offset in range(2, columns)], *arrived_slabs, begun)
    keep = keep + swap(send, (1, 1))
    for masks in zip(*exchange_rounds(bits(columns // 2, 2) + row_bits)):
        if masks[0][1] == 0:
            keep = keep + swap(keep, [mask[0] for mask in masks])
            continue
        far = swap(keep, [mask[1] for mask in masks])
        diagonal = swap(keep, [mask[0] ^ mask[1] for mask in masks])
        keep = (keep + swap(keep, [mask[0] for mask in masks])) + (far + diagonal)
    rest_of_gram = swap(keep, (1, 1))
    factor, directions = call(
        factor_kernel,
        (shape(f32, snaps, snaps), wide),
        [pltpu.VMEM((snaps, snaps), f32), span_scratch]
        + [pltpu.VMEM((snaps, snaps), f32)] * 2
        + [pltpu.VMEM((packed, LANES), f32)]
        + [pltpu.SemaphoreType.DMA((snaps // LANES,))] * 2,
        6 * snaps * snaps * points,
        16,
        stay=True,
    )(keep, rest_of_gram, high, rest)
    return (coefficients, factor, directions)


def solution(mesh):
    placed = (P("rows", "cols"), P(None, "rows"))
    return jax.shard_map(
        compute,
        mesh=mesh,
        in_specs=placed,
        out_specs=(P("cols", None), P(), P(None, ("rows", "cols"))),
        check_vma=False,
    )
```
